128 devices in a mesh: lon: 16 (over x, z_lo, core), lat: 8 (over y, z_hi).
Axes of the slice: x: 4, y: 4, z: 4 (z_hi: 2, z_lo: 2; z = z_hi * 2 + z_lo), core: 2. Of those that a mesh axis runs over, the one named last changes fastest.
Arguments:
- grid_state: bfloat16 [16, 8, 512, 227], P('lon', 'lat'), may hold values from -6 to 6
- grid_weight: bfloat16 [227, 512], replicated, may hold values from -0.375 to 0.375
- encode_weights: bfloat16 [2, 512, 512], replicated, may hold values from -0.25 to 0.25
- encode_bias: float32 [512], replicated, may hold values from -3 to 3
- mesh_gain: float32 [512], replicated, may hold values from 0.25 to 1.75
- g2m_sender: int32 [16, 8, 512], P('lon', 'lat'), may hold values from 0 to 511
- g2m_receiver: int32 [16, 8, 512], P('lon', 'lat'), may hold values from 0 to 255, as said below
- edge_geometry: float32 [16, 8, 4, 1536], P('lon', 'lat'), may hold values from -6 to 6
- edge_embed: float32 [4, 512], replicated, may hold values from -3 to 3
- mesh_sender: int32 [16, 8, 1536], P('lon', 'lat'), may hold values from 0 to 543, as said below
- mesh_receiver: int32 [16, 8, 1536], P('lon', 'lat'), may hold values from 0 to 255
- block_count: int32 [16, 8], P('lon', 'lat'), may hold values from 1 to 6, as said below
- export_nodes: int32 [16, 8, 32], P('lon', 'lat'), may hold values from 0 to 255, as said below
- proc_weights: bfloat16 [2, 7, 512, 512], replicated, may hold values from -0.25 to 0.25
- proc_bias: float32 [2, 2, 512], replicated, may hold values from -3 to 3
- proc_gain: float32 [2, 2, 512], replicated, may hold values from 0.25 to 1.75
- mesh_cotangent: bfloat16 [16, 8, 256, 512], P('lon', 'lat'), may hold values from -6 to 6
Outputs:
- mesh_latents: bfloat16 [16, 8, 256, 512], P('lon', 'lat')
- weight_grads: float32 [2, 128, 14336], P(None, ('lon', 'lat'))
- latent_grad: bfloat16 [16, 8, 256, 512], P('lon', 'lat')
The draws below stay inside these ranges and needn't reach their ends.
Inputs may be any that keep to these rules, and one draw needn't show every extreme that they name: `g2m_receiver`: every one of a device's 256 mesh nodes is the receiver of at least one of its grid-to-mesh edges. `mesh_sender`: an index below 256 names an own node; 256 + g * 32 + r names row r of export_nodes of the device v bands and w sectors away, g = 3 * (v + 1) + (w + 1), v and w in -1..1, never both 0, never beyond the first or last band; sectors wrap around. Blocks at or beyond block_count hold padding edges that are ignored. `export_nodes`: 32 different own nodes.
All inputs are finite; a program needn't handle non-finite values.
Results may differ from the reference program's by a relative error of at most 0.02.
Values may be sent and summed in bfloat16 or wider, within the bound.
No kernel may reach another device: no remote copies, remote signals or barrier semaphores. Data moves between devices by JAX's collectives and lax.ppermute only.
A program may use at most 128 MiB of HBM per device.

```python
from functools import partial
import jax
import jax.numpy as jnp
from jax import lax

D = 512
C = 227
M_DEV = 256
STEPS = 2
EDGE_BLOCK = 256
G_DEV = 512
B_DEV = 32
G2M_BLK = 2
E_CAP = 6
SECTORS = 16
BANDS = 8


def draw_g2m_receiver(key, part):
    edge_total = G2M_BLK * EDGE_BLOCK
    keys = jax.random.split(jax.random.fold_in(key, 11), SECTORS * BANDS)

    def one_device(device_key):
        first_key, second_key, third_key = jax.random.split(device_key, 3)
        covering = jax.random.permutation(first_key, M_DEV).astype(jnp.int32)
        filler = jax.random.randint(second_key, (edge_total - M_DEV,), 0, M_DEV, dtype=jnp.int32)
        joined = jnp.concatenate([covering, filler])
        return jnp.take(joined, jax.random.permutation(third_key, edge_total), axis=0)
    return jax.vmap(one_device)(keys).reshape(SECTORS, BANDS, edge_total).astype(jnp.int32)


def draw_mesh_sender(key, part):
    grid_shape = (SECTORS, BANDS, E_CAP * EDGE_BLOCK)
    first_key, second_key, third_key, fourth_key = jax.random.split(jax.random.fold_in(key, 23), 4)
    choose = jax.random.randint(first_key, grid_shape, 0, 5, dtype=jnp.int32)
    local_node = jax.random.randint(second_key, grid_shape, 0, M_DEV, dtype=jnp.int32)
    picked = jax.random.randint(third_key, grid_shape, 0, 8, dtype=jnp.int32)
    slot_index = picked + (picked >= 4).astype(jnp.int32)
    row_index = jax.random.randint(fourth_key, grid_shape, 0, B_DEV, dtype=jnp.int32)
    band_index = lax.broadcasted_iota(jnp.int32, grid_shape, 1)
    vertical = slot_index // 3 - 1
    lateral = slot_index % 3 - 1
    vertical = jnp.where((band_index == 0) & (vertical < 0), 1, vertical)
    vertical = jnp.where((band_index == BANDS - 1) & (vertical > 0), -1, vertical)
    slot_index = (vertical + 1) * 3 + lateral + 1
    remote = M_DEV + slot_index * B_DEV + row_index
    return jnp.where(choose < 3, local_node, remote).astype(jnp.int32)


def draw_block_count(key, part):
    band_index = lax.broadcasted_iota(jnp.int32, (SECTORS, BANDS), 1)
    sector_index = lax.broadcasted_iota(jnp.int32, (SECTORS, BANDS), 0)
    distance = jnp.abs(2 * band_index + 1 - BANDS)
    base_count = E_CAP - (distance - 1) * (E_CAP - 1) // max(BANDS - 2, 1)
    jitter = jax.random.randint(jax.random.fold_in(key, 31), (SECTORS, BANDS), 0, 2, dtype=jnp.int32)
    moved = jnp.where(base_count >= E_CAP, base_count - jitter, base_count + jitter)
    moved = jnp.where(sector_index == 0, base_count, moved)
    return jnp.clip(moved, 1, E_CAP).astype(jnp.int32)


def draw_export_nodes(key, part):
    keys = jax.random.split(jax.random.fold_in(key, 47), SECTORS * BANDS)

    def one_device(device_key):
        return jax.random.permutation(device_key, M_DEV)[:B_DEV].astype(jnp.int32)
    return jax.vmap(one_device)(keys).reshape(SECTORS, BANDS, B_DEV).astype(jnp.int32)


def set_ends(result, own_key, smallest, high):
    longest = result.shape.index(max(result.shape))
    spots = []
    for shift in (0, 1):
        where = [jax.random.randint(jax.random.fold_in(own_key, axis), (), 0, length) for axis, length in enumerate(result.shape)]
        where[longest] = (where[longest] + shift) % result.shape[longest]
        spots.append(tuple(where))
    return result.at[spots[0]].set(smallest).at[spots[1]].set(high)


def shard_levels(rng, extent, shards, least, top_value):
    level = 1.0
    for dim, shards_of in shards:
        draws = jax.random.uniform(jax.random.fold_in(jax.random.fold_in(rng, 6), dim), (shards_of,), jnp.float32, least / len(shards), top_value / len(shards))
        level = level * jnp.repeat(jnp.exp(draws), extent[dim] // shards_of).reshape((-1,) + (1,) * (len(extent) - 1 - dim))
    return level


def normal_values(key, dims, deviation, bound, pieces=(), kind=jnp.bfloat16):
    level = shard_levels(key, dims, pieces, -0.22, 0.18) if pieces else 1.0
    drawn = jax.random.normal(key, dims, jnp.float32) * deviation * level
    return jnp.minimum(jnp.maximum(drawn, -bound), bound).astype(kind)


def setup_inputs(seed: int = 0) -> dict:
    streams_of = jax.random.split(jax.random.key(seed), 18)
    return {
        "grid_state": normal_values(streams_of[0], (SECTORS, BANDS, G_DEV, C), 1.0, 6.0, ((0, 16), (1, 8))),
        "grid_weight": normal_values(streams_of[1], (C, D), C ** -0.5, 0.375),
        "encode_weights": normal_values(streams_of[2], (2, D, D), D ** -0.5, 0.25),
        "encode_bias": normal_values(streams_of[3], (D,), 0.5, 3.0, (), jnp.float32),
        "mesh_gain": jnp.clip(1.0 + 0.15 * jax.random.normal(streams_of[4], (D,), jnp.float32), 0.25, 1.75),
        "g2m_sender": set_ends(jax.random.randint(streams_of[5], (SECTORS, BANDS, G2M_BLK * EDGE_BLOCK), 0, G_DEV), jax.random.fold_in(streams_of[5], 1), 0, G_DEV - 1).astype(jnp.int32),
        "g2m_receiver": draw_g2m_receiver(jax.random.fold_in(streams_of[17], 71), 0),
        "edge_geometry": normal_values(streams_of[7], (SECTORS, BANDS, 4, E_CAP * EDGE_BLOCK), 1.0, 6.0, ((0, 16), (1, 8)), jnp.float32),
        "edge_embed": normal_values(streams_of[8], (4, D), 4 ** -0.5, 3.0, (), jnp.float32),
        "mesh_sender": draw_mesh_sender(jax.random.fold_in(streams_of[17], 71), 0),
        "mesh_receiver": set_ends(jax.random.randint(streams_of[10], (SECTORS, BANDS, E_CAP * EDGE_BLOCK), 0, M_DEV), jax.random.fold_in(streams_of[10], 1), 0, M_DEV - 1).astype(jnp.int32),
        "block_count": draw_block_count(jax.random.fold_in(streams_of[17], 71), 0),
        "export_nodes": draw_export_nodes(jax.random.fold_in(streams_of[17], 71), 0),
        "proc_weights": normal_values(streams_of[13], (STEPS, 7, D, D), D ** -0.5, 0.25),
        "proc_bias": normal_values(streams_of[14], (STEPS, 2, D), 0.5, 3.0, (), jnp.float32),
        "proc_gain": jnp.clip(1.0 + 0.15 * jax.random.normal(streams_of[15], (STEPS, 2, D), jnp.float32), 0.25, 1.75),
        "mesh_cotangent": normal_values(streams_of[16], (SECTORS, BANDS, M_DEV, D), 1.0, 6.0, ((0, 16), (1, 8))),
    }


EPSILON = 1e-05

def layer_norm(values):
    average = lax.optimization_barrier(jnp.mean(values, axis=-1, keepdims=True))
    centred = values - average
    variance = lax.optimization_barrier(jnp.mean(centred * centred, axis=-1, keepdims=True))
    return centred * lax.rsqrt(variance + EPSILON)

def encode(grid_rows, grid_weight, encode_weights, encode_bias, mesh_gain, g2m_sender, g2m_receiver, node_count):
    grid_latent = jax.nn.silu(jnp.dot(grid_rows, grid_weight, preferred_element_type=jnp.float32)).astype(jnp.bfloat16)
    projected = jnp.dot(grid_latent, encode_weights[0], preferred_element_type=jnp.float32)
    message_act = jax.nn.silu(jnp.take(projected, g2m_sender, axis=0) + encode_bias).astype(jnp.bfloat16)
    message = jnp.dot(message_act, encode_weights[1], preferred_element_type=jnp.float32).astype(jnp.bfloat16)
    onehot = (g2m_receiver[:, None] == jnp.arange(node_count, dtype=jnp.int32)[None, :]).astype(jnp.bfloat16)
    gathered = lax.dot_general(onehot, message, (((0,), (0,)), ((), ())), preferred_element_type=jnp.float32)
    return (layer_norm(gathered) * mesh_gain).astype(jnp.bfloat16)

def embed_edges(geometry, edge_embed):
    product = lax.dot_general(geometry, edge_embed, (((0,), (0,)), ((), ())), precision=lax.Precision.HIGHEST, preferred_element_type=jnp.float32)
    return product.astype(jnp.bfloat16)

def mesh_step(latent, halo_rows, edge_state, weights, sender, receiver, live_mask, bias, gain):
    node_count = latent.shape[0]
    extended = jnp.concatenate([latent, halo_rows], axis=0).astype(jnp.bfloat16)
    sender_proj = jnp.dot(extended, weights[1], preferred_element_type=jnp.float32)
    own_rows = latent.astype(jnp.bfloat16)
    receiver_proj = jnp.dot(own_rows, weights[2], preferred_element_type=jnp.float32)
    before = jnp.dot(edge_state, weights[0], preferred_element_type=jnp.float32)
    before = before + jnp.take(sender_proj, sender, axis=0) + jnp.take(receiver_proj, receiver, axis=0) + bias[0]
    edge_act = jax.nn.silu(before).astype(jnp.bfloat16)
    update = layer_norm(jnp.dot(edge_act, weights[3], preferred_element_type=jnp.float32)) * gain[0] * live_mask[:, None]
    new_edges = (edge_state.astype(jnp.float32) + update).astype(jnp.bfloat16)
    onehot = (receiver[:, None] == jnp.arange(node_count, dtype=jnp.int32)[None, :]).astype(jnp.bfloat16)
    node_sum = lax.dot_general(onehot, update.astype(jnp.bfloat16), (((0,), (0,)), ((), ())), preferred_element_type=jnp.float32).astype(jnp.bfloat16)
    inner = jnp.dot(own_rows, weights[4], preferred_element_type=jnp.float32)
    inner = inner + jnp.dot(node_sum, weights[5], preferred_element_type=jnp.float32) + bias[1]
    node_act = jax.nn.silu(inner).astype(jnp.bfloat16)
    new_latent = latent + layer_norm(jnp.dot(node_act, weights[6], preferred_element_type=jnp.float32)) * gain[1]
    return (new_latent, new_edges)

def band_shift(values, offset):
    if offset == 0:
        return values
    zero_rows = jnp.zeros_like(values[:, :1])
    if offset > 0:
        return jnp.concatenate([values[:, 1:], zero_rows], axis=1)
    return jnp.concatenate([zero_rows, values[:, :-1]], axis=1)

def assemble(latent32, export_nodes):
    exported = jax.vmap(jax.vmap(lambda rows_all, picked: jnp.take(rows_all, picked, axis=0)))(latent32, export_nodes)
    groups = []
    for vertical in (-1, 0, 1):
        for lateral in (-1, 0, 1):
            groups.append(band_shift(jnp.roll(exported, -lateral, axis=0), vertical))
    stacked = jnp.stack(groups, axis=2)
    return stacked.reshape(stacked.shape[:2] + (-1, stacked.shape[-1]))

def give_back(cot_rows):
    slots = cot_rows.reshape(cot_rows.shape[:2] + (3, 3, -1, cot_rows.shape[-1]))
    returned = jnp.zeros(slots.shape[:2] + slots.shape[4:], slots.dtype)
    for vertical in (-1, 0, 1):
        for lateral in (-1, 0, 1):
            moved = jnp.roll(slots[:, :, vertical + 1, lateral + 1], lateral, axis=0)
            returned = returned + band_shift(moved, -vertical)
    return returned

def reference(grid_state, grid_weight, encode_weights, encode_bias, mesh_gain, g2m_sender, g2m_receiver, edge_geometry, edge_embed, mesh_sender, mesh_receiver, block_count, export_nodes, proc_weights, proc_bias, proc_gain, mesh_cotangent):
    device_count = SECTORS * BANDS

    def flatten(values):
        return values.reshape((device_count,) + values.shape[2:])

    def unflatten(values):
        return values.reshape((SECTORS, BANDS) + values.shape[1:])

    def encode_device(entries):
        return encode(entries[0], grid_weight, encode_weights, encode_bias, mesh_gain, entries[1], entries[2], M_DEV)
    latent = lax.map(encode_device, (flatten(grid_state), flatten(g2m_sender), flatten(g2m_receiver)))
    edge_state = lax.map(partial(embed_edges, edge_embed=edge_embed), flatten(edge_geometry))
    block_of_edge = jnp.arange(E_CAP * EDGE_BLOCK, dtype=jnp.int32) // EDGE_BLOCK
    live_mask = (block_of_edge[None, :] < flatten(block_count)[:, None]).astype(jnp.float32)
    senders = flatten(mesh_sender)
    receivers = flatten(mesh_receiver)
    latent32 = lax.optimization_barrier(latent).astype(jnp.float32)
    records = []
    for step_index in range(STEPS):
        halo_rows = flatten(assemble(unflatten(latent32), export_nodes))

        def forward_device(entries):
            return mesh_step(entries[0], entries[1], entries[2], proc_weights[step_index], entries[3], entries[4], entries[5], proc_bias[step_index], proc_gain[step_index])
        new_latent, new_edges = lax.map(forward_device, (latent32, halo_rows, edge_state, senders, receivers, live_mask))
        records.append((latent32, halo_rows, edge_state))
        latent = new_latent.astype(jnp.bfloat16)
        latent32 = lax.optimization_barrier(latent).astype(jnp.float32)
        edge_state = new_edges
    cot_latent = flatten(mesh_cotangent).astype(jnp.float32)
    cot_edges = jnp.zeros_like(edge_state)
    totals = [None] * STEPS
    latent_gradient = None
    for step_index in reversed(range(STEPS)):

        def backward_device(carried, entries):
            local_step = partial(mesh_step, sender=entries[3], receiver=entries[4], live_mask=entries[5], bias=proc_bias[step_index], gain=proc_gain[step_index])
            unused, pullback = jax.vjp(local_step, entries[0], entries[1], entries[2], proc_weights[step_index])
            grad_latent, grad_halo, grad_edges, grad_weights = pullback((entries[6], entries[7]))
            return (carried + grad_weights.astype(jnp.float32), (grad_latent, grad_halo, grad_edges))
        saved_latent, saved_halo, saved_edges = records[step_index]
        summed, outputs = lax.scan(backward_device, jnp.zeros(proc_weights.shape[1:], jnp.float32), (saved_latent, saved_halo, saved_edges, senders, receivers, live_mask, cot_latent, cot_edges))
        grad_latent, grad_halo, grad_edges = outputs
        totals[step_index] = summed
        returned = give_back(unflatten(grad_halo))
        added = jax.vmap(jax.vmap(lambda grads_all, picked, extra_rows: grads_all.at[picked].add(extra_rows)))(unflatten(grad_latent), export_nodes, returned)
        rounded = flatten(added).astype(jnp.bfloat16)
        latent_gradient = rounded
        cot_latent = lax.optimization_barrier(rounded).astype(jnp.float32)
        cot_edges = grad_edges
    weight_grads = jnp.stack(totals).reshape(STEPS, device_count, -1)
    return (unflatten(latent), weight_grads, unflatten(latent_gradient))
```

```python
import jax
import jax.numpy as jnp
from jax import lax
from jax.experimental import pallas as pl
from jax.experimental.pallas import tpu as pltpu
from jax.sharding import PartitionSpec as P

EDGE_BLOCK = 256
EPSILON = 1e-05
F32 = jnp.float32
BF16 = jnp.bfloat16
HIGHEST = lax.Precision.HIGHEST


def dot(a, b):
    return jnp.dot(a, b, preferred_element_type=F32)


def dot_nt(a, b):
    return lax.dot_general(a, b, (((1,), (1,)), ((), ())), preferred_element_type=F32)


def dot_tn(a, b):
    return lax.dot_general(a, b, (((0,), (0,)), ((), ())), preferred_element_type=F32)


def gate(v):
    return 0.5 * jnp.tanh(0.5 * v) + 0.5


def silu(v):
    return v * gate(v)


def silu_slope(v):
    s = gate(v)
    return s * (1.0 + v * (1.0 - s))


def norm(v):
    mean = jnp.mean(v, axis=-1, keepdims=True)
    centred = v - mean
    variance = jnp.mean(centred * centred, axis=-1, keepdims=True)
    scale = lax.rsqrt(variance + EPSILON)
    return centred * scale, scale


def norm_back(g, y, scale):
    first = jnp.mean(g, axis=-1, keepdims=True)
    second = jnp.mean(g * y, axis=-1, keepdims=True)
    return scale * (g - first - y * second)


def ids_down(row, count, base=0):
    shape = (count, row.shape[1])
    numbers = (lax.broadcasted_iota(jnp.int32, shape, 0) + base).astype(F32)
    return jnp.where(numbers == row.astype(F32), 1.0, 0.0).astype(BF16)


def ids_across(row, count, base=0):
    edges = row.shape[1]
    column = jnp.transpose(jnp.broadcast_to(row.astype(F32), (128, edges)))
    parts = []
    lane = lax.broadcasted_iota(jnp.int32, (edges, 128), 1).astype(F32)
    for start in range(0, count, 128):
        width = min(128, count - start)
        hit = jnp.where(column == lane + float(start + base), 1.0, 0.0)
        parts.append(hit[:, :width])
    return jnp.concatenate(parts, axis=1).astype(BF16)


VMEM_SPEC = pl.BlockSpec(memory_space=pltpu.VMEM)
SMEM_SPEC = pl.BlockSpec(memory_space=pltpu.SMEM)


def call(body, outs, args, smem=(), scratch=(), flops=10**9, name=None, limit=44):
    touched = sum(a.size * a.dtype.itemsize for a in args) + sum(
        o.size * o.dtype.itemsize for o in outs
    )
    return pl.pallas_call(
        body,
        out_shape=tuple(outs),
        in_specs=[SMEM_SPEC if i in smem else VMEM_SPEC for i in range(len(args))],
        out_specs=tuple(VMEM_SPEC for _ in outs),
        scratch_shapes=list(scratch),
        compiler_params=pltpu.CompilerParams(vmem_limit_bytes=limit << 20),
        cost_estimate=pl.CostEstimate(flops=flops, bytes_accessed=touched, transcendentals=0),
        name=name,
    )(*args)


def shape(dims, dtype):
    return jax.ShapeDtypeStruct(dims, dtype)


def encode_body(grid, gw, ew, eb, gain, sender, receiver, exports, latent_out, export_out):
    cells = grid.shape[0]
    nodes = latent_out.shape[0]
    latent = silu(dot(grid[...], gw[...])).astype(BF16)
    total = jnp.zeros(latent_out.shape, F32)
    edges = sender.shape[1]
    for start in range(0, edges, 256):
        part = slice(start, start + 256)
        picked = dot(ids_across(sender[:, part], cells), latent).astype(BF16)
        act = silu(dot(picked, ew[0]) + eb[...]).astype(BF16)
        message = dot(act, ew[1]).astype(BF16)
        total = total + dot(ids_down(receiver[:, part], nodes), message)
    value = (norm(total)[0] * gain[...]).astype(BF16)
    latent_out[...] = value
    export_out[...] = dot(ids_across128(exports[...], nodes), value).astype(BF16)


def ids_across128(row, count):
    return ids_across(row, count)[:32]


def pre_body(latent, edge_state, weights, bias, sender, receiver, pre_out):
    nodes = latent.shape[0]
    own = jnp.concatenate(
        [dot(latent[...], weights[1]), dot(latent[...], weights[2])], axis=0
    ).astype(BF16)
    for start in range(0, sender.shape[1], EDGE_BLOCK):
        part = slice(start, start + EDGE_BLOCK)
        picks = jnp.concatenate(
            [ids_across(sender[:, part], nodes), ids_across(receiver[:, part], nodes)], axis=1
        )
        pre_out[part] = dot(edge_state[part], weights[0]) + dot(picks, own) + bias[0:1]


def edges_forward(
    pre, halo, weights, gain, sender, receiver, count, before_out, act_out, y_out, scale_out, nodes
):
    rim = dot(halo[...], weights[1]).astype(BF16)
    total = jnp.zeros((nodes, halo.shape[1]), F32)
    updates = []
    for block in range(sender.shape[1] // EDGE_BLOCK):
        part = slice(block * EDGE_BLOCK, (block + 1) * EDGE_BLOCK)
        live = (block < count[0, 0]).astype(F32)
        before = pre[part] + dot(ids_across(sender[:, part], halo.shape[0], nodes), rim)
        before_out[part] = before
        act = silu(before).astype(BF16)
        act_out[part] = act
        y, scale = norm(dot(act, weights[3]))
        y_out[part] = y.astype(y_out.dtype)
        scale_out[part] = jnp.broadcast_to(scale, (EDGE_BLOCK, 128))
        update = y * (gain[0:1] * live)
        updates.append(update)
        total = total + dot(ids_down(receiver[:, part], nodes), update.astype(BF16))
    return total.astype(BF16), updates


def nodes_forward(latent, node_sum, weights, bias, gain):
    inner = dot(latent, weights[4]) + dot(node_sum, weights[5]) + bias[1:2]
    act = silu(inner).astype(BF16)
    z, scale = norm(dot(act, weights[6]))
    return inner, act, z, scale, latent.astype(F32) + z * gain[1:2]


def forward_body(
    pre, halo, latent, edge_state, weights, bias, gain, sender, receiver, exports, count,
    latent_out, export_out, edges_out, before_out, act_out, y_out, scale_out,
    sum_out, inner_out, nact_out, z_out, nscale_out,
):
    nodes = latent.shape[0]
    node_sum, updates = edges_forward(
        pre, halo, weights, gain, sender, receiver, count, before_out, act_out, y_out, scale_out,
        nodes,
    )
    for block, update in enumerate(updates):
        part = slice(block * EDGE_BLOCK, (block + 1) * EDGE_BLOCK)
        edges_out[part] = (edge_state[part].astype(F32) + update).astype(BF16)
    inner, act, z, scale, new = nodes_forward(latent[...], node_sum, weights, bias, gain)
    value = new.astype(BF16)
    latent_out[...] = value
    export_out[...] = dot(ids_across128(exports[...], nodes), value).astype(BF16)
    sum_out[...] = node_sum
    inner_out[...] = inner
    nact_out[...] = act
    z_out[...] = z
    nscale_out[...] = jnp.broadcast_to(scale, nscale_out.shape)


def nodes_backward(cot, inner, z, scale, weights, gain):
    dq = norm_back(cot * gain[1:2], z, scale).astype(BF16)
    dact = dot_nt(dq, weights[6]).astype(BF16).astype(F32)
    dinner = (dact * silu_slope(inner)).astype(BF16)
    dsum = dot_nt(dinner, weights[5]).astype(BF16)
    return dq, dinner, dsum


def edges_backward(
    dsum, edge_cot, before, act, y, scale, weights, gain, receiver, count, dh_out, dbefore_out
):
    nodes = dsum.shape[0]
    for block in range(receiver.shape[1] // EDGE_BLOCK):
        part = slice(block * EDGE_BLOCK, (block + 1) * EDGE_BLOCK)
        live = (block < count[0, 0]).astype(F32)
        cot = dot(ids_across(receiver[:, part], nodes), dsum)
        if edge_cot is not None:
            cot = cot + edge_cot[part].astype(F32)
        dh = norm_back(cot * (gain[0:1] * live), y[part].astype(F32), scale[part][:, 0:1])
        dh = dh.astype(BF16)
        dh_out[part] = dh
        dact = dot_nt(dh, weights[3]).astype(BF16).astype(F32)
        dbefore_out[part] = (dact * silu_slope(before[part])).astype(BF16)


def halo_back(dbefore, sender, weights, nodes, slots, out):
    total = jnp.zeros((slots, dbefore.shape[1]), F32)
    for block in range(sender.shape[1] // EDGE_BLOCK):
        part = slice(block * EDGE_BLOCK, (block + 1) * EDGE_BLOCK)
        total = total + dot(ids_down(sender[:, part], slots, nodes), dbefore[part])
    total = total.astype(BF16)
    out[...] = dot_nt(total, weights[1]).astype(BF16)
    return total


def last_body(
    pre, halo, latent, weights, bias, gain, sender, receiver, cotangent, count,
    latent_out, halo_out, act_out, dh_out, dbefore_out, drim_out, sum_out, nact_out, dq_out, dinner_out,
    before, y, scale,
):
    nodes = latent.shape[0]
    node_sum, _ = edges_forward(
        pre, halo, weights, gain, sender, receiver, count, before, act_out, y, scale, nodes
    )
    inner, nact, z, nscale, new = nodes_forward(latent[...], node_sum, weights, bias, gain)
    latent_out[...] = new.astype(BF16)
    sum_out[...] = node_sum
    nact_out[...] = nact
    dq, dinner, dsum = nodes_backward(
        cotangent[...].astype(F32), inner, z, nscale, weights, gain
    )
    dq_out[...] = dq
    dinner_out[...] = dinner
    edges_backward(
        dsum, None, before, act_out, y, scale, weights, gain, receiver, count, dh_out, dbefore_out
    )
    drim_out[...] = halo_back(dbefore_out, sender, weights, nodes, halo.shape[0], halo_out)


def weight_parts(
    latent, halo, node_sum, nact, edge_state, act, dq, dinner, dh, dbefore, drim, weights, sender,
    receiver, base, grads_out, edge_cot_out,
):
    nodes = latent.shape[0]
    dsend = jnp.zeros((nodes, latent.shape[1]), F32)
    drecv = jnp.zeros((nodes, latent.shape[1]), F32)
    for block in range(sender.shape[1] // EDGE_BLOCK):
        part = slice(block * EDGE_BLOCK, (block + 1) * EDGE_BLOCK)
        dsend = dsend + dot(ids_down(sender[:, part], nodes), dbefore[part])
        drecv = drecv + dot(ids_down(receiver[:, part], nodes), dbefore[part])
    dsend = dsend.astype(BF16)
    drecv = drecv.astype(BF16)
    rows = latent[...]
    grads_out[6] = dot_tn(nact[...], dq[...]).astype(BF16)
    grads_out[5] = dot_tn(node_sum[...], dinner[...]).astype(BF16)
    grads_out[4] = dot_tn(rows, dinner[...]).astype(BF16)
    grads_out[3] = dot_tn(act[...], dh[...]).astype(BF16)
    grads_out[2] = dot_tn(rows, drecv).astype(BF16)
    grads_out[1] = (dot_tn(rows, dsend) + dot_tn(halo[...], drim[...])).astype(BF16)
    grads_out[0] = dot_tn(edge_state[...], dbefore[...]).astype(BF16)
    if edge_cot_out is not None:
        edge_cot_out[...] = dot_nt(dbefore[...], weights[0]).astype(BF16)
    own = (
        dot_nt(dinner[...], weights[4]).astype(BF16).astype(F32)
        + dot_nt(drecv, weights[2]).astype(BF16).astype(F32)
    ).astype(BF16).astype(F32)
    return base + own + dot_nt(dsend, weights[1]).astype(BF16).astype(F32)


def weights_body(
    latent, halo, node_sum, nact, edge_state, act, dq, dinner, dh, dbefore, drim, weights, sender,
    receiver, cotangent, grads_out, edge_cot_out, latent_cot_out,
):
    latent_cot_out[...] = weight_parts(
        latent, halo, node_sum, nact, edge_state, act, dq, dinner, dh, dbefore, drim, weights,
        sender, receiver, cotangent[...].astype(F32), grads_out, edge_cot_out,
    )


def add_returned(cot, returned, exports):
    spots = ids_across128(exports, cot.shape[0]).astype(F32)
    extra = lax.dot_general(
        spots, returned, (((0,), (0,)), ((), ())), precision=HIGHEST, preferred_element_type=F32
    )
    return (cot + extra).astype(BF16)


def first_body(
    latent_cot, returned, edge_cot, latent, halo, edge_state, weights, gain, sender, receiver, exports,
    before, act, y, scale, node_sum, inner, nact, z, nscale, count,
    grads_out, halo_out, latent_cot_out,
    dh, dbefore,
):
    nodes = latent.shape[0]
    cot = add_returned(latent_cot[...], returned[...], exports[...]).astype(F32)
    dq, dinner, dsum = nodes_backward(
        cot, inner[...], z[...], nscale[...][:, 0:1], weights, gain
    )
    edges_backward(
        dsum, edge_cot, before, act, y, scale, weights, gain, receiver, count, dh, dbefore
    )
    drim = halo_back(dbefore, sender, weights, nodes, halo.shape[0], halo_out)
    latent_cot_out[...] = weight_parts(
        latent, halo, node_sum, nact, edge_state, act, dq, dinner, dh, dbefore, drim, weights,
        sender, receiver, cot, grads_out, None,
    )


def finish_body(latent_cot, returned, exports, out):
    out[...] = add_returned(latent_cot[...], returned[...], exports[...])


def neighbours(axis, wrap):
    size = lax.axis_size(axis)
    up = [(i, (i + 1) % size) for i in range(size if wrap else size - 1)]
    return up, [(j, i) for i, j in up]


def exchange(rows):
    up, down = neighbours("lon", True)
    rims = jnp.concatenate(
        [lax.ppermute(rows, "lon", up), rows, lax.ppermute(rows, "lon", down)], axis=0
    )
    up, down = neighbours("lat", False)
    return jnp.concatenate(
        [lax.ppermute(rims, "lat", up), rims, lax.ppermute(rims, "lat", down)], axis=0
    )


def give_back(cot):
    slots = cot.reshape(3, 3, -1, cot.shape[-1])
    up, down = neighbours("lon", True)
    from_before = lax.ppermute(slots[:, 2], "lon", up)
    from_after = lax.ppermute(slots[:, 0], "lon", down)
    bands = slots[:, 1].astype(F32) + from_before.astype(F32) + from_after.astype(F32)
    up, down = neighbours("lat", False)
    low = lax.ppermute(bands[2].astype(BF16), "lat", up)
    high = lax.ppermute(bands[0].astype(BF16), "lat", down)
    return bands[1] + low.astype(F32) + high.astype(F32)


def reduce_pieces(grads):
    sectors, bands = lax.axis_size("lon"), lax.axis_size("lat")
    width = grads.shape[-1]
    half = sectors // 2
    by_core = grads.reshape(half, 2, -1, width)
    core = lax.axis_index("lon") % 2
    keep = lax.dynamic_index_in_dim(by_core, core, 1, False)
    send = lax.dynamic_index_in_dim(by_core, 1 - core, 1, False)
    other = lax.ppermute(send, "lon", [(i, i ^ 1) for i in range(sectors)])
    pair = (keep.astype(F32) + other.astype(F32)).astype(BF16)
    groups = [
        [(2 * s + c) * bands + b for s in range(half) for b in range(bands)] for c in range(2)
    ]
    pieces = lax.all_to_all(
        pair.reshape(half * bands, -1, width), ("lon", "lat"), 0, 0, axis_index_groups=groups,
        tiled=True,
    )
    return jnp.sum(pieces.astype(F32), axis=0).reshape(1, -1)


def shards(
    grid_state, grid_weight, encode_weights, encode_bias, mesh_gain, g2m_sender, g2m_receiver,
    edge_geometry, edge_embed, mesh_sender, mesh_receiver, block_count, export_nodes, proc_weights,
    proc_bias, proc_gain, mesh_cotangent,
):
    nodes, width = mesh_cotangent.shape[2:]
    sender, receiver = mesh_sender[0], mesh_receiver[0]
    edges = sender.shape[1]
    exports = jnp.pad(export_nodes[0], ((0, 0), (0, 128 - export_nodes.shape[2])))
    cotangent = mesh_cotangent[0, 0]
    node16 = shape((nodes, width), BF16)
    node32 = shape((nodes, width), F32)
    edge16 = shape((edges, width), BF16)
    edge32 = shape((edges, width), F32)
    rows16 = shape(exports.shape[:1] + (width,), BF16)
    rows16 = shape((export_nodes.shape[2], width), BF16)
    slots = 9 * export_nodes.shape[2]
    halo16 = shape((slots, width), BF16)
    scale32 = shape((edges, 128), F32)

    latent0, export0 = call(
        encode_body, (node16, rows16),
        (grid_state[0, 0], grid_weight, encode_weights, encode_bias[None], mesh_gain[None],
         g2m_sender[0], g2m_receiver[0], exports),
        name="encode",
    )
    halo0 = exchange(export0)
    edge0 = lax.dot_general(
        edge_geometry[0, 0], edge_embed, (((0,), (0,)), ((), ())), precision=HIGHEST,
        preferred_element_type=F32,
    ).astype(BF16)
    weights, bias, gain = proc_weights, proc_bias, proc_gain
    (pre0,) = call(
        pre_body, (edge32,), (latent0, edge0, weights[0], bias[0], sender, receiver),
        flops=3 * 10**9, name="pre0",
    )
    (latent1, export1, edge1, before0, act0, y0, scale0, sum0, inner0, nact0, z0, nscale0) = call(
        forward_body,
        (node16, rows16, edge16, edge32, edge16, edge16, scale32, node16, node32, node16, node32,
         shape((nodes, 128), F32)),
        (pre0, halo0, latent0, edge0, weights[0], bias[0], gain[0], sender, receiver, exports,
         block_count),
        smem=(10,), flops=3 * 10**9, name="forward0",
    )
    halo1 = exchange(export1)
    (pre1,) = call(
        pre_body, (edge32,), (latent1, edge1, weights[1], bias[1], sender, receiver),
        flops=3 * 10**9, name="pre1",
    )
    (latent2, dhalo1, act1, dh1, dbefore1, drim1, sum1, nact1, dq1, dinner1) = call(
        last_body,
        (node16, halo16, edge16, edge16, edge16, halo16, node16, node16, node16, node16),
        (pre1, halo1, latent1, weights[1], bias[1], gain[1], sender, receiver, cotangent,
         block_count),
        smem=(9,),
        scratch=(pltpu.VMEM((edges, width), F32), pltpu.VMEM((edges, width), F32),
                 pltpu.VMEM((edges, 128), F32)),
        flops=6 * 10**9, name="last",
    )
    returned1 = give_back(dhalo1)
    grads1, edge_cot1, latent_cot1 = call(
        weights_body, (shape((7, width, width), BF16), edge16, node32),
        (latent1, halo1, sum1, nact1, edge1, act1, dq1, dinner1, dh1, dbefore1, drim1, weights[1],
         sender, receiver, cotangent),
        flops=6 * 10**9, name="weights1",
    )
    piece1 = reduce_pieces(grads1)
    grads0, dhalo0, latent_cot0 = call(
        first_body, (shape((7, width, width), BF16), halo16, node32),
        (latent_cot1, returned1, edge_cot1, latent0, halo0, edge0, weights[0], gain[0], sender,
         receiver, exports, before0, act0, y0, scale0, sum0, inner0, nact0, z0, nscale0,
         block_count),
        smem=(20,),
        scratch=(pltpu.VMEM((edges, width), BF16), pltpu.VMEM((edges, width), BF16)),
        flops=9 * 10**9, name="backward0",
    )
    returned0 = give_back(dhalo0)
    piece0 = reduce_pieces(grads0)
    (latent_grad,) = call(
        finish_body, (node16,), (latent_cot0, returned0, exports), name="finish",
    )
    weight_grads = jnp.stack([piece0, piece1])
    return latent2[None, None], weight_grads, latent_grad[None, None]


def solution(mesh):
    tile = P("lon", "lat", None)
    deep = P("lon", "lat", None, None)
    return jax.shard_map(
        shards,
        mesh=mesh,
        in_specs=(
            deep, P(), P(), P(), P(), tile, tile, deep, P(), tile, tile, P("lon", "lat"), tile,
            P(), P(), P(), deep,
        ),
        out_specs=(deep, P(None, ("lon", "lat"), None), deep),
        check_vma=False,
    )
```

```python
from functools import partial

import jax
import jax.numpy as jnp
from jax import lax
from jax.experimental import pallas as pl
from jax.experimental.pallas import tpu as pltpu
from jax.sharding import PartitionSpec as P

EDGE_BLOCK = 256
EPSILON = 1e-05
F32 = jnp.float32
BF16 = jnp.bfloat16
HIGHEST = lax.Precision.HIGHEST


def dot(a, b):
    return jnp.dot(a, b, preferred_element_type=F32)


def dot_nt(a, b):
    return lax.dot_general(a, b, (((1,), (1,)), ((), ())), preferred_element_type=F32)


def dot_tn(a, b):
    return lax.dot_general(a, b, (((0,), (0,)), ((), ())), preferred_element_type=F32)


def gate(v):
    return 0.5 * jnp.tanh(0.5 * v) + 0.5


def silu(v):
    return v * gate(v)


def silu_slope(v):
    s = gate(v)
    return s * (1.0 + v * (1.0 - s))


def norm(v):
    mean = jnp.mean(v, axis=-1, keepdims=True)
    centred = v - mean
    variance = jnp.mean(centred * centred, axis=-1, keepdims=True)
    scale = lax.rsqrt(variance + EPSILON)
    return centred * scale, scale


def norm_back(g, y, scale):
    first = jnp.mean(g, axis=-1, keepdims=True)
    second = jnp.mean(g * y, axis=-1, keepdims=True)
    return scale * (g - first - y * second)


def ids_down(row, count, base=0):
    shape = (count, row.shape[1])
    numbers = (lax.broadcasted_iota(jnp.int32, shape, 0) + base).astype(F32)
    return jnp.where(numbers == row.astype(F32), 1.0, 0.0).astype(BF16)


def ids_across(row, count, base=0):
    edges = row.shape[1]
    column = jnp.transpose(jnp.broadcast_to(row.astype(F32), (128, edges)))
    parts = []
    lane = lax.broadcasted_iota(jnp.int32, (edges, 128), 1).astype(F32)
    for start in range(0, count, 128):
        width = min(128, count - start)
        hit = jnp.where(column == lane + float(start + base), 1.0, 0.0)
        parts.append(hit[:, :width])
    return jnp.concatenate(parts, axis=1).astype(BF16)


VMEM_SPEC = pl.BlockSpec(memory_space=pltpu.VMEM)
SMEM_SPEC = pl.BlockSpec(memory_space=pltpu.SMEM)
HBM_SPEC = pl.BlockSpec(memory_space=pltpu.HBM)
ANY_SPEC = pl.BlockSpec(memory_space=pl.ANY)
SPECS = {"v": VMEM_SPEC, "s": SMEM_SPEC, "h": HBM_SPEC, "a": ANY_SPEC}
MATRICES = 7


def call(body, name, args, outs, scratch=(), out_kinds=None, limit=24, flops=10**6):
    out_kinds = out_kinds or "v" * len(outs)
    return pl.pallas_call(
        body,
        out_shape=tuple(outs),
        in_specs=[SPECS[kind] for _, kind in args],
        out_specs=tuple(SPECS[kind] for kind in out_kinds),
        scratch_shapes=list(scratch),
        compiler_params=pltpu.CompilerParams(vmem_limit_bytes=limit << 20),
        cost_estimate=pl.CostEstimate(flops=flops, bytes_accessed=10**5, transcendentals=0),
        name=name,
    )(*[a for a, _ in args])


def shape(dims, dtype):
    return jax.ShapeDtypeStruct(dims, dtype)


class Fetch:
    def __init__(self, source, step, order, held, sems):
        self.place = {m: j for j, m in enumerate(order)}
        self.held = held
        self.pending = {}
        for m, j in self.place.items():
            copy = pltpu.make_async_copy(source.at[step, m], held.at[j], sems.at[j])
            copy.start()
            self.pending[m] = copy

    def __getitem__(self, m):
        copy = self.pending.pop(m, None)
        if copy is not None:
            copy.wait()
        return self.held[self.place[m]]


def fetch_scratch(order, width):
    return (pltpu.VMEM((len(order), width, width), BF16), pltpu.SemaphoreType.DMA((len(order),)))


def encode_body(
    grid_in, gw_in, ew_in, eb_in, gain_in, sender_in, receiver_in, exports_in,
    latent_out, export_out,
    grid, gw, ew, eb, gain, sender, receiver, exports, sems,
):
    pairs = [
        (grid_in, grid), (gw_in, gw), (sender_in, sender), (ew_in, ew), (eb_in, eb),
        (receiver_in, receiver), (gain_in, gain), (exports_in, exports),
    ]
    copies = [pltpu.make_async_copy(a, b, sems.at[i]) for i, (a, b) in enumerate(pairs)]
    for copy in copies:
        copy.start()
    copies[0].wait()
    copies[1].wait()
    cells = grid.shape[1]
    nodes = latent_out.shape[0]
    latent = silu(dot_tn(grid[...], gw[...])).astype(BF16)
    for copy in copies[2:]:
        copy.wait()
    total = jnp.zeros(latent_out.shape, F32)
    edges = sender.shape[1]
    for start in range(0, edges, 256):
        part = slice(start, start + 256)
        picked = dot(ids_across(sender[:, part], cells), latent).astype(BF16)
        act = silu(dot(picked, ew[0]) + eb[...]).astype(BF16)
        message = dot(act, ew[1]).astype(BF16)
        total = total + dot(ids_down(receiver[:, part], nodes), message)
    value = (norm(total)[0] * gain[...]).astype(BF16)
    latent_out[...] = value
    export_out[...] = dot_tn(ids_down(exports[...], nodes), value).astype(BF16)


PRE_ORDER = (1, 2, 0)


def embed_edges(geometry, embed):
    features, edges = geometry.shape
    columns = [
        jnp.transpose(jnp.broadcast_to(geometry[f : f + 1], (128, edges))) for f in range(features)
    ]
    parts = []
    for start in range(0, embed.shape[1], 128):
        total = columns[0] * embed[0:1, start : start + 128]
        for f in range(1, features):
            total = total + columns[f] * embed[f : f + 1, start : start + 128]
        parts.append(total)
    return jnp.concatenate(parts, axis=1)


def first_pre_body(
    geometry, embed, latent, weights_in, bias, sender, receiver, edge_out, pre_out, held, sems
):
    values = embed[...]
    for start in range(0, sender.shape[1], EDGE_BLOCK):
        part = slice(start, start + EDGE_BLOCK)
        edge_out[part] = embed_edges(geometry[:, part], values).astype(BF16)
    pre_body(0, latent, edge_out, weights_in, bias, sender, receiver, pre_out, held, sems)


def pre_body(step, latent, edge_state, weights_in, bias, sender, receiver, pre_out, held, sems):
    weights = Fetch(weights_in, step, PRE_ORDER, held, sems)
    nodes = latent.shape[0]
    rows = latent[...]
    own = jnp.concatenate([dot(rows, weights[1]), dot(rows, weights[2])], axis=0).astype(BF16)
    for start in range(0, sender.shape[1], EDGE_BLOCK):
        part = slice(start, start + EDGE_BLOCK)
        picks = jnp.concatenate(
            [ids_across(sender[:, part], nodes), ids_across(receiver[:, part], nodes)], axis=1
        )
        pre_out[part] = dot(edge_state[part], weights[0]) + dot(picks, own) + bias[step, 0:1]


def band_masks():
    band = lax.axis_index("lat")
    return (band > 0).astype(F32), (band < lax.axis_size("lat") - 1).astype(F32)


def halo_rows(before, own, after):
    count = before.shape[0] // 3
    low, high = (mask.astype(BF16) for mask in band_masks())
    parts = []
    for v, mask in ((0, low), (1, None), (2, high)):
        for ref in (before, own, after):
            rows = ref[v * count : (v + 1) * count]
            parts.append(rows if mask is None else rows * mask)
    return jnp.concatenate(parts, axis=0)


def edges_forward(
    step, pre, halo, weights, gain, sender, receiver, count, slope_out, act_out, y_out, scale_out, nodes
):
    rim = dot(halo, weights[1]).astype(BF16)
    total = jnp.zeros((nodes, halo.shape[1]), F32)
    updates = []
    for block in range(sender.shape[1] // EDGE_BLOCK):
        part = slice(block * EDGE_BLOCK, (block + 1) * EDGE_BLOCK)
        live = (block < count[0, 0]).astype(F32)
        before = pre[part] + dot(ids_across(sender[:, part], halo.shape[0], nodes), rim)
        share = gate(before)
        value = before * share
        slope_out[part] = (share + value - value * share).astype(BF16)
        act = value.astype(BF16)
        act_out[part] = act
        y, scale = norm(dot(act, weights[3]))
        y_out[part] = y.astype(BF16)
        scale_out[part] = jnp.broadcast_to(scale, (EDGE_BLOCK, 128))
        update = y * (gain[step, 0:1] * live)
        updates.append(update)
        total = total + dot(ids_down(receiver[:, part], nodes), update.astype(BF16))
    return total.astype(BF16), updates


def nodes_forward(step, latent, node_sum, weights, bias, gain):
    inner = dot(latent, weights[4]) + dot(node_sum, weights[5]) + bias[step, 1:2]
    act = silu(inner).astype(BF16)
    z, scale = norm(dot(act, weights[6]))
    return inner, act, z, scale, latent.astype(F32) + z * gain[step, 1:2]


FORWARD_ORDER = (1, 3, 4, 5, 6)


def forward_body(
    pre, halo_before, halo_own, halo_after, latent, edge_state, weights_in, bias, gain, sender,
    receiver, exports, count,
    latent_out, export_out, edges_out, slope_out, act_out, y_out, scale_out,
    sum_out, inner_out, nact_out, z_out, nscale_out,
    held, sems,
):
    weights = Fetch(weights_in, 0, FORWARD_ORDER, held, sems)
    nodes = latent.shape[0]
    halo = halo_rows(halo_before, halo_own, halo_after)
    node_sum, updates = edges_forward(
        0, pre, halo, weights, gain, sender, receiver, count, slope_out, act_out, y_out, scale_out,
        nodes,
    )
    for block, update in enumerate(updates):
        part = slice(block * EDGE_BLOCK, (block + 1) * EDGE_BLOCK)
        edges_out[part] = (edge_state[part].astype(F32) + update).astype(BF16)
    inner, act, z, scale, new = nodes_forward(0, latent[...], node_sum, weights, bias, gain)
    value = new.astype(BF16)
    latent_out[...] = value
    export_out[...] = dot_tn(ids_down(exports[...], nodes), value).astype(BF16)
    sum_out[...] = node_sum
    inner_out[...] = inner
    nact_out[...] = act
    z_out[...] = z
    nscale_out[...] = jnp.broadcast_to(scale, nscale_out.shape)


def nodes_backward(step, cot, inner, z, scale, weights, gain):
    dq = norm_back(cot * gain[step, 1:2], z, scale).astype(BF16)
    dact = dot_nt(dq, weights[6]).astype(BF16).astype(F32)
    dinner = (dact * silu_slope(inner)).astype(BF16)
    dsum = dot_nt(dinner, weights[5]).astype(BF16)
    return dq, dinner, dsum


def edges_backward(
    step, dsum, edge_cot, slope, y, scale, weights, gain, receiver, count, dh_out, dbefore_out
):
    nodes = dsum.shape[0]
    for block in range(receiver.shape[1] // EDGE_BLOCK):
        part = slice(block * EDGE_BLOCK, (block + 1) * EDGE_BLOCK)
        live = (block < count[0, 0]).astype(F32)
        cot = dot(ids_across(receiver[:, part], nodes), dsum)
        if edge_cot is not None:
            cot = cot + edge_cot[part].astype(F32)
        dh = norm_back(cot * (gain[step, 0:1] * live), y[part].astype(F32), scale[part][:, 0:1])
        dh = dh.astype(BF16)
        dh_out[part] = dh
        dact = dot_nt(dh, weights[3]).astype(BF16).astype(F32)
        dbefore_out[part] = (dact * slope[part].astype(F32)).astype(BF16)


def halo_back(dbefore, sender, weights, nodes, outs):
    rows = outs[0].shape[0] // 3
    slots = 9 * rows
    total = jnp.zeros((slots, dbefore.shape[1]), F32)
    for block in range(sender.shape[1] // EDGE_BLOCK):
        part = slice(block * EDGE_BLOCK, (block + 1) * EDGE_BLOCK)
        total = total + dot(ids_down(sender[:, part], slots, nodes), dbefore[part])
    total = total.astype(BF16)
    grad = dot_nt(total, weights[1]).astype(BF16)
    for v in range(3):
        for w in range(3):
            g = 3 * v + w
            outs[w][v * rows : (v + 1) * rows] = grad[g * rows : (g + 1) * rows]
    return total


LAST_ORDER = (1, 3, 4, 5, 6)


def last_body(
    pre, halo_before, halo_own, halo_after, latent, weights_in, bias, gain, sender, receiver,
    cotangent, count,
    latent_out, back_before, back_own, back_after, act_out, dh_out, dbefore_out, drim_out, sum_out,
    nact_out, dq_out, dinner_out,
    slope, y, scale, held, sems,
):
    weights = Fetch(weights_in, 1, LAST_ORDER, held, sems)
    nodes = latent.shape[0]
    halo = halo_rows(halo_before, halo_own, halo_after)
    node_sum, _ = edges_forward(
        1, pre, halo, weights, gain, sender, receiver, count, slope, act_out, y, scale, nodes
    )
    inner, nact, z, nscale, new = nodes_forward(1, latent[...], node_sum, weights, bias, gain)
    latent_out[...] = new.astype(BF16)
    sum_out[...] = node_sum
    nact_out[...] = nact
    dq, dinner, dsum = nodes_backward(
        1, cotangent[...].astype(F32), inner, z, nscale, weights, gain
    )
    dq_out[...] = dq
    dinner_out[...] = dinner
    edges_backward(
        1, dsum, None, slope, y, scale, weights, gain, receiver, count, dh_out, dbefore_out
    )
    drim_out[...] = halo_back(
        dbefore_out, sender, weights, nodes, (back_before, back_own, back_after)
    )


def weights_body(
    step, latent, halo_before, halo_own, halo_after, node_sum, nact, edge_state, act, dq, dinner, dh,
    dbefore, drim, weights_in, sender, receiver, cotangent, *rest,
):
    if step:
        keep_out, send_out, edge_cot_out, latent_cot_out = rest[:4]
        order = (0, 4, 2, 1)
    else:
        keep_out, send_out, latent_cot_out = rest[:3]
        order = (4, 2, 1)
    held, sems, total, pieces, piece_sems = rest[-5:]
    weights = Fetch(weights_in, step, order, held, sems)
    nodes, width = latent.shape
    halves, bands, tall = pieces.shape[1:4]
    rows_of = MATRICES * width // (2 * halves * bands)
    mine = lax.axis_index("lon") % 2
    copies = []
    emitted = 0

    spare = tall - rows_of
    number = lax.broadcasted_iota(jnp.int32, (tall, width), 0)
    inside = number >= spare if step else number < rows_of
    edge = jnp.zeros((8, width), F32)
    total[:8] = edge
    total[8 + MATRICES * width :] = edge

    def put(matrix, value):
        nonlocal emitted
        total[8 + matrix * width : 8 + (matrix + 1) * width] = value
        ready = (matrix + 1) * width + (spare if matrix == MATRICES - 1 else 0)
        while emitted < 2 * halves and ((emitted + 1) * bands - 1) * rows_of + tall <= ready:
            for band in range(bands):
                first = 8 + (emitted * bands + band) * rows_of - (spare if step else 0)
                rows = jnp.where(inside, total[first : first + tall], 0.0)
                pieces[emitted % 2, emitted // 2, band] = rows.astype(BF16)
            emitted += 1
            if emitted % 2 == 0:
                h = emitted // 2 - 1
                for place, out in ((mine, keep_out), (1 - mine, send_out)):
                    copy = pltpu.make_async_copy(
                        pieces.at[place, h], out.at[h], piece_sems.at[len(copies)]
                    )
                    copy.start()
                    copies.append(copy)

    rows = latent[...]
    put(0, dot_tn(edge_state[...], dbefore[...]))
    dsend = jnp.zeros((nodes, width), F32)
    drecv = jnp.zeros((nodes, width), F32)
    for block in range(sender.shape[1] // EDGE_BLOCK):
        part = slice(block * EDGE_BLOCK, (block + 1) * EDGE_BLOCK)
        dsend = dsend + dot(ids_down(sender[:, part], nodes), dbefore[part])
        drecv = drecv + dot(ids_down(receiver[:, part], nodes), dbefore[part])
    dsend = dsend.astype(BF16)
    drecv = drecv.astype(BF16)
    halo = halo_rows(halo_before, halo_own, halo_after)
    put(1, dot_tn(rows, dsend) + dot_tn(halo, drim[...]))
    put(2, dot_tn(rows, drecv))
    put(3, dot_tn(act[...], dh[...]))
    put(4, dot_tn(rows, dinner[...]))
    put(5, dot_tn(node_sum[...], dinner[...]))
    put(6, dot_tn(nact[...], dq[...]))
    if step:
        edge_cot_out[...] = dot_nt(dbefore[...], weights[0]).astype(BF16)
    own = (
        dot_nt(dinner[...], weights[4]).astype(BF16).astype(F32)
        + dot_nt(drecv, weights[2]).astype(BF16).astype(F32)
    ).astype(BF16).astype(F32)
    latent_cot_out[...] = (
        cotangent[...].astype(F32) + own + dot_nt(dsend, weights[1]).astype(BF16).astype(F32)
    )
    for copy in copies:
        copy.wait()


def add_returned(cot, own, before, after, exports):
    spots = ids_down(exports, cot.shape[0]).astype(F32)
    low, high = band_masks()
    returned = own + before.astype(F32) * low + after.astype(F32) * high
    extra = jnp.dot(spots, returned, precision=HIGHEST, preferred_element_type=F32)
    return (cot + extra).astype(BF16)


BACKWARD_ORDER = (6, 5, 3, 1)


def backward_body(
    latent_cot, back_own_in, back_low, back_high, edge_cot, weights_in, gain, sender, receiver, exports, slope, y, scale,
    inner, z, nscale, count,
    back_before, back_own, back_after, dh_out, dbefore_out, drim_out, dq_out, dinner_out, cot_out,
    held, sems,
):
    weights = Fetch(weights_in, 0, BACKWARD_ORDER, held, sems)
    nodes = latent_cot.shape[0]
    cot16 = add_returned(
        latent_cot[...], back_own_in[...], back_low[...], back_high[...], exports[...]
    )
    cot_out[...] = cot16
    dq, dinner, dsum = nodes_backward(
        0, cot16.astype(F32), inner[...], z[...], nscale[...][:, 0:1], weights, gain
    )
    dq_out[...] = dq
    dinner_out[...] = dinner
    edges_backward(
        0, dsum, edge_cot, slope, y, scale, weights, gain, receiver, count, dh_out, dbefore_out
    )
    drim_out[...] = halo_back(
        dbefore_out, sender, weights, nodes, (back_before, back_own, back_after)
    )


def finish_body(latent_cot, back_own_in, back_low, back_high, exports, out):
    out[...] = add_returned(
        latent_cot[...], back_own_in[...], back_low[...], back_high[...], exports[...]
    )


def neighbours(axis, wrap):
    size = lax.axis_size(axis)
    up = [(i, (i + 1) % size) for i in range(size if wrap else size - 1)]
    return up, [(j, i) for i, j in up]


def stack_body(low, own, high, out):
    rows = own.shape[0]
    for v, ref in enumerate((low, own, high)):
        out[v * rows : (v + 1) * rows] = ref[...]


def combine_body(own, from_before, from_after, low_out, own_out, high_out):
    rows = own_out.shape[0]
    total = own[...].astype(F32) + from_before[...].astype(F32) + from_after[...].astype(F32)
    low_out[...] = total[:rows].astype(BF16)
    own_out[...] = total[rows : 2 * rows]
    high_out[...] = total[2 * rows :].astype(BF16)


def exchange(rows):
    up, down = neighbours("lat", True)
    parts = (lax.ppermute(rows, "lat", up), rows, lax.ppermute(rows, "lat", down))
    kind = shape((3 * rows.shape[0], rows.shape[1]), BF16)
    (bands,) = call(stack_body, "stack", [(p, "v") for p in parts], (kind,))
    up, down = neighbours("lon", True)
    return lax.ppermute(bands, "lon", up), bands, lax.ppermute(bands, "lon", down)


def give_back(before, own, after):
    up, down = neighbours("lon", True)
    from_before = lax.ppermute(after, "lon", up)
    from_after = lax.ppermute(before, "lon", down)
    rows = own.shape[0] // 3
    to_low, kept, to_high = call(
        combine_body, "combine", [(own, "v"), (from_before, "v"), (from_after, "v")],
        (shape((rows, own.shape[1]), BF16), shape((rows, own.shape[1]), F32),
         shape((rows, own.shape[1]), BF16)),
    )
    up, down = neighbours("lat", True)
    low = lax.ppermute(to_high, "lat", up)
    high = lax.ppermute(to_low, "lat", down)
    return kept, low, high


def join_body(rows_of, keep0, other0, keep1, other1, out):
    halves, bands, tall, width = keep0.shape
    lap = 2 * (tall - rows_of)
    for h in range(halves):
        for band in range(bands):
            first = keep0[h, band].astype(F32) + other0[h, band].astype(F32)
            second = keep1[h, band].astype(F32) + other1[h, band].astype(F32)
            middle = first[tall - lap :] + second[:lap]
            block = jnp.concatenate([first[: tall - lap], middle, second[lap:]], axis=0)
            out[h * bands + band] = block.astype(BF16)


def swap_cores(send):
    sectors = lax.axis_size("lon")
    return lax.ppermute(send, "lon", [(i, i ^ 1) for i in range(sectors)])


def reduce_pieces(joined):
    sectors, bands = lax.axis_size("lon"), lax.axis_size("lat")
    groups = [
        [(2 * s + c) * bands + b for s in range(sectors // 2) for b in range(bands)]
        for c in range(2)
    ]
    pieces = lax.all_to_all(
        joined, ("lon", "lat"), 0, 0, axis_index_groups=groups, tiled=True
    )
    return jnp.sum(pieces.astype(F32), axis=0).reshape(2, 1, -1)


def shards(
    grid_state, grid_weight, encode_weights, encode_bias, mesh_gain, g2m_sender, g2m_receiver,
    edge_geometry, edge_embed, mesh_sender, mesh_receiver, block_count, export_nodes, proc_weights,
    proc_bias, proc_gain, mesh_cotangent,
):
    nodes, width = mesh_cotangent.shape[2:]
    sectors, bands = lax.axis_size("lon"), lax.axis_size("lat")
    sender, receiver, exports = mesh_sender[0], mesh_receiver[0], export_nodes[0]
    edges, exported = sender.shape[1], exports.shape[1]
    cotangent = mesh_cotangent[0, 0]
    node16 = shape((nodes, width), BF16)
    node32 = shape((nodes, width), F32)
    edge16 = shape((edges, width), BF16)
    edge32 = shape((edges, width), F32)
    rows16 = shape((exported, width), BF16)
    band16 = shape((3 * exported, width), BF16)
    slots16 = shape((9 * exported, width), BF16)
    scale32 = shape((edges, 128), F32)
    rows_of = MATRICES * width // (sectors * bands)
    tall = -(-rows_of // 16) * 16
    half16 = shape((sectors // 2, bands, tall, width), BF16)

    sources = (
        jnp.swapaxes(grid_state[0, 0], 0, 1), grid_weight, encode_weights, encode_bias[None], mesh_gain[None],
        g2m_sender[0], g2m_receiver[0], exports,
    )
    latent0, export0 = call(
        encode_body, "encode", [(a, "h") for a in sources], (node16, rows16),
        scratch=[pltpu.VMEM(a.shape, a.dtype) for a in sources] + [pltpu.SemaphoreType.DMA((8,))],
        limit=56,
    )
    halo0 = exchange(export0)
    def weight_grads_of(step, latent, halo, node_sum, nact, edge_state, act, dq, dinner, dh, dbefore,
                        drim, cot):
        order = (0, 4, 2, 1) if step else (4, 2, 1)
        return call(
            partial(weights_body, step), "weights",
            [(a, "v") for a in (latent,) + halo + (node_sum, nact, edge_state, act, dq, dinner, dh,
                                                  dbefore, drim)]
            + [(proc_weights, "h"), (sender, "v"), (receiver, "v"), (cot, "v")],
            (half16, half16) + ((edge16,) if step else ()) + (node32,),
            out_kinds="aa" + ("v" if step else "") + "v",
            scratch=fetch_scratch(order, width) + (
                pltpu.VMEM((MATRICES * width + 16, width), F32),
                pltpu.VMEM((2,) + half16.shape, BF16),
                pltpu.SemaphoreType.DMA((sectors,)),
            ),
            flops=6 * 10**9,
        )

    shared = [(proc_weights, "h"), (proc_bias, "v"), (sender, "v"), (receiver, "v")]
    edge0, pre0 = call(
        first_pre_body, "first_pre",
        [(edge_geometry[0, 0], "v"), (edge_embed, "v"), (latent0, "v")] + shared,
        (edge16, edge32), scratch=fetch_scratch(PRE_ORDER, width), flops=5 * 10**9,
    )
    (latent1, export1, edge1, slope0, act0, y0, scale0, sum0, inner0, nact0, z0, nscale0) = call(
        forward_body, "forward",
        [(pre0, "v")] + [(h, "v") for h in halo0]
        + [(latent0, "v"), (edge0, "v"), (proc_weights, "h"), (proc_bias, "v"), (proc_gain, "v"),
           (sender, "v"), (receiver, "v"), (exports, "v"), (block_count, "s")],
        (node16, rows16, edge16, edge16, edge16, edge16, scale32, node16, node32, node16, node32,
         shape((nodes, 128), F32)),
        scratch=fetch_scratch(FORWARD_ORDER, width),
    )
    halo1 = exchange(export1)
    (pre1,) = call(
        partial(pre_body, 1), "pre", [(latent1, "v"), (edge1, "v")] + shared, (edge32,),
        scratch=fetch_scratch(PRE_ORDER, width), flops=3 * 10**9,
    )
    (latent2, before1, own1, after1, act1, dh1, dbefore1, drim1, sum1, nact1, dq1, dinner1) = call(
        last_body, "last",
        [(pre1, "v")] + [(h, "v") for h in halo1]
        + [(latent1, "v"), (proc_weights, "h"), (proc_bias, "v"), (proc_gain, "v"), (sender, "v"),
           (receiver, "v"), (cotangent, "v"), (block_count, "s")],
        (node16, band16, band16, band16, edge16, edge16, edge16, slots16, node16, node16, node16,
         node16),
        scratch=(pltpu.VMEM((edges, width), BF16), pltpu.VMEM((edges, width), BF16),
                 pltpu.VMEM((edges, 128), F32)) + fetch_scratch(LAST_ORDER, width),
    )
    returned1 = give_back(before1, own1, after1)
    keep1, send1, edge_cot1, latent_cot1 = weight_grads_of(
        1, latent1, halo1, sum1, nact1, edge1, act1, dq1, dinner1, dh1, dbefore1, drim1, cotangent
    )
    other1 = swap_cores(send1)
    (before0, own0, after0, dh0, dbefore0, drim0, dq0, dinner0, cot0) = call(
        backward_body, "backward",
        [(latent_cot1, "v")] + [(r, "v") for r in returned1] + [(edge_cot1, "v"), (proc_weights, "h"),
         (proc_gain, "v"), (sender, "v"), (receiver, "v"), (exports, "v"), (slope0, "v"),
         (y0, "v"), (scale0, "v"), (inner0, "v"), (z0, "v"), (nscale0, "v"), (block_count, "s")],
        (band16, band16, band16, edge16, edge16, slots16, node16, node16, node16),
        scratch=fetch_scratch(BACKWARD_ORDER, width),
    )
    returned0 = give_back(before0, own0, after0)
    keep0, send0, latent_cot0 = weight_grads_of(
        0, latent0, halo0, sum0, nact0, edge0, act0, dq0, dinner0, dh0, dbefore0, drim0, cot0
    )
    other0 = swap_cores(send0)
    (joined,) = call(
        partial(join_body, rows_of), "join",
        [(keep0, "v"), (other0, "v"), (keep1, "v"), (other1, "v")],
        (shape((sectors // 2 * bands, 2 * rows_of, width), BF16),),
    )
    joined, returned0 = lax.optimization_barrier((joined, returned0))
    weight_grads = reduce_pieces(joined)
    (latent_grad,) = call(
        finish_body, "finish", [(latent_cot0, "v")] + [(r, "v") for r in returned0] + [(exports, "v")], (node16,)
    )
    return latent2[None, None], weight_grads, latent_grad[None, None]


def solution(mesh):
    tile = P("lon", "lat", None)
    deep = P("lon", "lat", None, None)
    return jax.shard_map(
        shards,
        mesh=mesh,
        in_specs=(
            deep, P(), P(), P(), P(), tile, tile, deep, P(), tile, tile, P("lon", "lat"), tile,
            P(), P(), P(), deep,
        ),
        out_specs=(deep, P(None, ("lon", "lat"), None), deep),
        check_vma=False,
    )
```

```python
from functools import partial

import jax
import jax.numpy as jnp
from jax import lax
from jax.experimental import pallas as pl
from jax.experimental.pallas import tpu as pltpu
from jax.sharding import PartitionSpec as P

EDGE_BLOCK = 256
EPSILON = 1e-05
F32 = jnp.float32
BF16 = jnp.bfloat16
HIGHEST = lax.Precision.HIGHEST


def dot(a, b):
    return jnp.dot(a, b, preferred_element_type=F32)


def dot_nt(a, b):
    return lax.dot_general(a, b, (((1,), (1,)), ((), ())), preferred_element_type=F32)


def dot_tn(a, b):
    return lax.dot_general(a, b, (((0,), (0,)), ((), ())), preferred_element_type=F32)


def gate(v):
    return 0.5 * jnp.tanh(0.5 * v) + 0.5


def silu(v):
    return v * gate(v)


def silu_slope(v):
    s = gate(v)
    return s * (1.0 + v * (1.0 - s))


def norm(v):
    mean = jnp.mean(v, axis=-1, keepdims=True)
    centred = v - mean
    variance = jnp.mean(centred * centred, axis=-1, keepdims=True)
    scale = lax.rsqrt(variance + EPSILON)
    return centred * scale, scale


def norm_back(g, y, scale):
    first = jnp.mean(g, axis=-1, keepdims=True)
    second = jnp.mean(g * y, axis=-1, keepdims=True)
    return scale * (g - first - y * second)


def ids_down(row, count, base=0):
    shape = (count, row.shape[1])
    numbers = (lax.broadcasted_iota(jnp.int32, shape, 0) + base).astype(F32)
    return jnp.where(numbers == row.astype(F32), 1.0, 0.0).astype(BF16)


def ids_across(row, count, base=0):
    edges = row.shape[1]
    column = jnp.transpose(jnp.broadcast_to(row.astype(F32), (128, edges)))
    parts = []
    lane = lax.broadcasted_iota(jnp.int32, (edges, 128), 1).astype(F32)
    for start in range(0, count, 128):
        width = min(128, count - start)
        hit = jnp.where(column == lane + float(start + base), 1.0, 0.0)
        parts.append(hit[:, :width])
    return jnp.concatenate(parts, axis=1).astype(BF16)


VMEM_SPEC = pl.BlockSpec(memory_space=pltpu.VMEM)
SMEM_SPEC = pl.BlockSpec(memory_space=pltpu.SMEM)
HBM_SPEC = pl.BlockSpec(memory_space=pltpu.HBM)
ANY_SPEC = pl.BlockSpec(memory_space=pl.ANY)
SPECS = {"v": VMEM_SPEC, "s": SMEM_SPEC, "h": HBM_SPEC, "a": ANY_SPEC}
MATRICES = 7


def call(body, name, args, outs, scratch=(), out_kinds=None, limit=24, flops=10**6):
    out_kinds = out_kinds or "v" * len(outs)
    return pl.pallas_call(
        body,
        out_shape=tuple(outs),
        in_specs=[SPECS[kind] for _, kind in args],
        out_specs=tuple(SPECS[kind] for kind in out_kinds),
        scratch_shapes=list(scratch),
        compiler_params=pltpu.CompilerParams(vmem_limit_bytes=limit << 20),
        cost_estimate=pl.CostEstimate(flops=flops, bytes_accessed=10**5, transcendentals=0),
        name=name,
    )(*[a for a, _ in args])


def shape(dims, dtype):
    return jax.ShapeDtypeStruct(dims, dtype)


class Fetch:
    def __init__(self, source, step, order, held, sems):
        self.place = {m: j for j, m in enumerate(order)}
        self.held = held
        self.pending = {}
        for m, j in self.place.items():
            copy = pltpu.make_async_copy(source.at[step, m], held.at[j], sems.at[j])
            copy.start()
            self.pending[m] = copy

    def __getitem__(self, m):
        copy = self.pending.pop(m, None)
        if copy is not None:
            copy.wait()
        return self.held[self.place[m]]


def fetch_scratch(order, width):
    return (pltpu.VMEM((len(order), width, width), BF16), pltpu.SemaphoreType.DMA((len(order),)))


def encode_body(
    grid_in, gw_in, ew_in, eb_in, gain_in, sender_in, receiver_in, exports_in,
    latent_out, export_out,
    grid, gw, ew, eb, gain, sender, receiver, exports, sems,
):
    pairs = [
        (grid_in, grid), (gw_in, gw), (sender_in, sender), (ew_in, ew), (eb_in, eb),
        (receiver_in, receiver), (gain_in, gain), (exports_in, exports),
    ]
    copies = [pltpu.make_async_copy(a, b, sems.at[i]) for i, (a, b) in enumerate(pairs)]
    for copy in copies:
        copy.start()
    copies[0].wait()
    copies[1].wait()
    cells = grid.shape[1]
    nodes = latent_out.shape[0]
    latent = silu(dot_tn(grid[...], gw[...])).astype(BF16)
    for copy in copies[2:]:
        copy.wait()
    total = jnp.zeros(latent_out.shape, F32)
    edges = sender.shape[1]
    for start in range(0, edges, 256):
        part = slice(start, start + 256)
        picked = dot(ids_across(sender[:, part], cells), latent).astype(BF16)
        act = silu(dot(picked, ew[0]) + eb[...]).astype(BF16)
        message = dot(act, ew[1]).astype(BF16)
        total = total + dot(ids_down(receiver[:, part], nodes), message)
    value = (norm(total)[0] * gain[...]).astype(BF16)
    latent_out[...] = value
    export_out[...] = dot_tn(ids_down(exports[...], nodes), value).astype(BF16)


PRE_ORDER = (1, 2, 0)


def embed_edges(geometry, embed):
    features, edges = geometry.shape
    columns = [
        jnp.transpose(jnp.broadcast_to(geometry[f : f + 1], (128, edges))) for f in range(features)
    ]
    parts = []
    for start in range(0, embed.shape[1], 128):
        total = columns[0] * embed[0:1, start : start + 128]
        for f in range(1, features):
            total = total + columns[f] * embed[f : f + 1, start : start + 128]
        parts.append(total)
    return jnp.concatenate(parts, axis=1)


def first_pre_body(
    geometry, embed, latent, weights_in, bias, sender, receiver, edge_out, pre_out, held, sems
):
    values = embed[...]
    for start in range(0, sender.shape[1], EDGE_BLOCK):
        part = slice(start, start + EDGE_BLOCK)
        edge_out[part] = embed_edges(geometry[:, part], values).astype(BF16)
    pre_body(0, latent, edge_out, weights_in, bias, sender, receiver, pre_out, held, sems)


def pre_body(step, latent, edge_state, weights_in, bias, sender, receiver, pre_out, held, sems):
    weights = Fetch(weights_in, step, PRE_ORDER, held, sems)
    nodes = latent.shape[0]
    rows = latent[...]
    own = jnp.concatenate([dot(rows, weights[1]), dot(rows, weights[2])], axis=0).astype(BF16)
    for start in range(0, sender.shape[1], EDGE_BLOCK):
        part = slice(start, start + EDGE_BLOCK)
        picks = jnp.concatenate(
            [ids_across(sender[:, part], nodes), ids_across(receiver[:, part], nodes)], axis=1
        )
        pre_out[part] = dot(edge_state[part], weights[0]) + dot(picks, own) + bias[step, 0:1]


def band_masks():
    band = lax.axis_index("lat")
    return (band > 0).astype(F32), (band < lax.axis_size("lat") - 1).astype(F32)


def halo_rows(before, own, after):
    count = before.shape[0] // 3
    low, high = (mask.astype(BF16) for mask in band_masks())
    parts = []
    for v, mask in ((0, low), (1, None), (2, high)):
        for ref in (before, own, after):
            rows = ref[v * count : (v + 1) * count]
            parts.append(rows if mask is None else rows * mask)
    return jnp.concatenate(parts, axis=0)


def edges_forward(
    step, pre, halo, weights, gain, sender, receiver, count, slope_out, act_out, y_out, scale_out, nodes,
    edges=None,
):
    rim = dot(halo, weights[1]).astype(BF16)
    blocks = sender.shape[1] // EDGE_BLOCK
    parts = [slice(b * EDGE_BLOCK, (b + 1) * EDGE_BLOCK) for b in range(blocks)]
    total = jnp.zeros((nodes, halo.shape[1]), F32)
    before, hidden, update = {}, {}, {}

    def project(b):
        before[b] = dot(ids_across(sender[:, parts[b]], halo.shape[0], nodes), rim)

    def activate(b):
        value = pre[parts[b]] + before.pop(b)
        share = gate(value)
        product = value * share
        slope_out[parts[b]] = (share + product - product * share).astype(BF16)
        act_out[parts[b]] = product.astype(BF16)

    def multiply(b):
        hidden[b] = dot(act_out[parts[b]], weights[3])

    def finish(b):
        live = (b < count[0, 0]).astype(F32)
        y, scale = norm(hidden.pop(b))
        y_out[parts[b]] = y.astype(BF16)
        scale_out[parts[b]] = jnp.broadcast_to(scale, (EDGE_BLOCK, 128))
        value = y * (gain[step, 0:1] * live)
        update[b] = value.astype(BF16)
        if edges is not None:
            edges[1][parts[b]] = (edges[0][parts[b]].astype(F32) + value).astype(BF16)

    project(0)
    for b in range(blocks + 2):
        if b + 1 < blocks:
            project(b + 1)
        if b < blocks:
            activate(b)
        if 1 <= b <= blocks:
            finish(b - 1) if b - 1 in hidden else None
        if b < blocks:
            multiply(b)
        if b >= 1 and b - 1 in update:
            total = total + dot(ids_down(receiver[:, parts[b - 1]], nodes), update.pop(b - 1))
    return total.astype(BF16)


def nodes_forward(step, latent, node_sum, weights, bias, gain):
    inner = dot(latent, weights[4]) + dot(node_sum, weights[5]) + bias[step, 1:2]
    act = silu(inner).astype(BF16)
    z, scale = norm(dot(act, weights[6]))
    return inner, act, z, scale, latent.astype(F32) + z * gain[step, 1:2]


FORWARD_ORDER = (1, 3, 4, 5, 6)


def forward_body(
    pre, halo_before, halo_own, halo_after, latent, edge_state, weights_in, bias, gain, sender,
    receiver, exports, count,
    latent_out, export_out, edges_out, slope_out, act_out, y_out, scale_out,
    sum_out, inner_out, nact_out, z_out, nscale_out,
    held, sems,
):
    weights = Fetch(weights_in, 0, FORWARD_ORDER, held, sems)
    nodes = latent.shape[0]
    halo = halo_rows(halo_before, halo_own, halo_after)
    node_sum = edges_forward(
        0, pre, halo, weights, gain, sender, receiver, count, slope_out, act_out, y_out, scale_out,
        nodes, (edge_state, edges_out),
    )
    inner, act, z, scale, new = nodes_forward(0, latent[...], node_sum, weights, bias, gain)
    value = new.astype(BF16)
    latent_out[...] = value
    export_out[...] = dot_tn(ids_down(exports[...], nodes), value).astype(BF16)
    sum_out[...] = node_sum
    inner_out[...] = inner
    nact_out[...] = act
    z_out[...] = z
    nscale_out[...] = jnp.broadcast_to(scale, nscale_out.shape)


def nodes_backward(step, cot, inner, z, scale, weights, gain):
    dq = norm_back(cot * gain[step, 1:2], z, scale).astype(BF16)
    dact = dot_nt(dq, weights[6]).astype(BF16).astype(F32)
    dinner = (dact * silu_slope(inner)).astype(BF16)
    dsum = dot_nt(dinner, weights[5]).astype(BF16)
    return dq, dinner, dsum


def edges_backward(
    step, dsum, edge_cot, slope, y, scale, weights, gain, receiver, count, dh_out, dbefore_out
):
    nodes = dsum.shape[0]
    blocks = receiver.shape[1] // EDGE_BLOCK
    parts = [slice(b * EDGE_BLOCK, (b + 1) * EDGE_BLOCK) for b in range(blocks)]
    cots, dacts = {}, {}

    def spread(b):
        cots[b] = dot(ids_across(receiver[:, parts[b]], nodes), dsum)

    def through_norm(b):
        live = (b < count[0, 0]).astype(F32)
        cot = cots.pop(b)
        if edge_cot is not None:
            cot = cot + edge_cot[parts[b]].astype(F32)
        dh = norm_back(
            cot * (gain[step, 0:1] * live), y[parts[b]].astype(F32), scale[parts[b]][:, 0:1]
        )
        dh_out[parts[b]] = dh.astype(BF16)

    def multiply(b):
        dacts[b] = dot_nt(dh_out[parts[b]], weights[3])

    def finish(b):
        dact = dacts.pop(b).astype(BF16).astype(F32)
        dbefore_out[parts[b]] = (dact * slope[parts[b]].astype(F32)).astype(BF16)

    spread(0)
    for b in range(blocks + 1):
        if b + 1 < blocks:
            spread(b + 1)
        if b < blocks:
            through_norm(b)
        if b >= 1:
            finish(b - 1)
        if b < blocks:
            multiply(b)


def halo_back(dbefore, sender, weights, nodes, outs):
    rows = outs[0].shape[0] // 3
    slots = 9 * rows
    total = jnp.zeros((slots, dbefore.shape[1]), F32)
    for block in range(sender.shape[1] // EDGE_BLOCK):
        part = slice(block * EDGE_BLOCK, (block + 1) * EDGE_BLOCK)
        total = total + dot(ids_down(sender[:, part], slots, nodes), dbefore[part])
    total = total.astype(BF16)
    grad = dot_nt(total, weights[1]).astype(BF16)
    for v in range(3):
        for w in range(3):
            g = 3 * v + w
            outs[w][v * rows : (v + 1) * rows] = grad[g * rows : (g + 1) * rows]
    return total


LAST_ORDER = (1, 3, 4, 5, 6)


def last_body(
    pre, halo_before, halo_own, halo_after, latent, weights_in, bias, gain, sender, receiver,
    cotangent, count,
    latent_out, back_before, back_own, back_after, act_out, dh_out, dbefore_out, drim_out, sum_out,
    nact_out, dq_out, dinner_out,
    slope, y, scale, held, sems,
):
    weights = Fetch(weights_in, 1, LAST_ORDER, held, sems)
    nodes = latent.shape[0]
    halo = halo_rows(halo_before, halo_own, halo_after)
    node_sum = edges_forward(
        1, pre, halo, weights, gain, sender, receiver, count, slope, act_out, y, scale, nodes
    )
    inner, nact, z, nscale, new = nodes_forward(1, latent[...], node_sum, weights, bias, gain)
    latent_out[...] = new.astype(BF16)
    sum_out[...] = node_sum
    nact_out[...] = nact
    dq, dinner, dsum = nodes_backward(
        1, cotangent[...].astype(F32), inner, z, nscale, weights, gain
    )
    dq_out[...] = dq
    dinner_out[...] = dinner
    edges_backward(
        1, dsum, None, slope, y, scale, weights, gain, receiver, count, dh_out, dbefore_out
    )
    drim_out[...] = halo_back(
        dbefore_out, sender, weights, nodes, (back_before, back_own, back_after)
    )


def weights_body(
    step, latent, halo_before, halo_own, halo_after, node_sum, nact, edge_state, act, dq, dinner, dh,
    dbefore, drim, weights_in, sender, receiver, cotangent, *rest,
):
    if step:
        keep_out, send_out, edge_cot_out, latent_cot_out = rest[:4]
        order = (0, 4, 2, 1)
    else:
        keep_out, send_out, latent_cot_out = rest[:3]
        order = (4, 2, 1)
    held, sems, total, pieces, piece_sems = rest[-5:]
    weights = Fetch(weights_in, step, order, held, sems)
    nodes, width = latent.shape
    halves, bands, tall = pieces.shape[1:4]
    rows_of = MATRICES * width // (2 * halves * bands)
    mine = lax.axis_index("lon") % 2
    copies = []
    emitted = 0

    spare = tall - rows_of
    number = lax.broadcasted_iota(jnp.int32, (tall, width), 0)
    inside = number >= spare if step else number < rows_of
    edge = jnp.zeros((8, width), F32)
    total[:8] = edge
    total[8 + MATRICES * width :] = edge

    def put(matrix, value):
        nonlocal emitted
        total[8 + matrix * width : 8 + (matrix + 1) * width] = value
        ready = (matrix + 1) * width + (spare if matrix == MATRICES - 1 else 0)
        while emitted < 2 * halves and ((emitted + 1) * bands - 1) * rows_of + tall <= ready:
            for band in range(bands):
                first = 8 + (emitted * bands + band) * rows_of - (spare if step else 0)
                rows = jnp.where(inside, total[first : first + tall], 0.0)
                pieces[emitted % 2, emitted // 2, band] = rows.astype(BF16)
            emitted += 1
            if emitted % 2 == 0:
                h = emitted // 2 - 1
                for place, out in ((mine, keep_out), (1 - mine, send_out)):
                    copy = pltpu.make_async_copy(
                        pieces.at[place, h], out.at[h], piece_sems.at[len(copies)]
                    )
                    copy.start()
                    copies.append(copy)

    rows = latent[...]
    put(0, dot_tn(edge_state[...], dbefore[...]))
    dsend = jnp.zeros((nodes, width), F32)
    drecv = jnp.zeros((nodes, width), F32)
    for block in range(sender.shape[1] // EDGE_BLOCK):
        part = slice(block * EDGE_BLOCK, (block + 1) * EDGE_BLOCK)
        dsend = dsend + dot(ids_down(sender[:, part], nodes), dbefore[part])
        drecv = drecv + dot(ids_down(receiver[:, part], nodes), dbefore[part])
    dsend = dsend.astype(BF16)
    drecv = drecv.astype(BF16)
    halo = halo_rows(halo_before, halo_own, halo_after)
    put(1, dot_tn(rows, dsend) + dot_tn(halo, drim[...]))
    put(2, dot_tn(rows, drecv))
    put(3, dot_tn(act[...], dh[...]))
    put(4, dot_tn(rows, dinner[...]))
    put(5, dot_tn(node_sum[...], dinner[...]))
    put(6, dot_tn(nact[...], dq[...]))
    if step:
        edge_cot_out[...] = dot_nt(dbefore[...], weights[0]).astype(BF16)
    own = (
        dot_nt(dinner[...], weights[4]).astype(BF16).astype(F32)
        + dot_nt(drecv, weights[2]).astype(BF16).astype(F32)
    ).astype(BF16).astype(F32)
    latent_cot_out[...] = (
        cotangent[...].astype(F32) + own + dot_nt(dsend, weights[1]).astype(BF16).astype(F32)
    )
    for copy in copies:
        copy.wait()


def add_returned(cot, own, before, after, exports):
    spots = ids_down(exports, cot.shape[0]).astype(F32)
    low, high = band_masks()
    returned = own + before.astype(F32) * low + after.astype(F32) * high
    extra = jnp.dot(spots, returned, precision=HIGHEST, preferred_element_type=F32)
    return (cot + extra).astype(BF16)


BACKWARD_ORDER = (6, 5, 3, 1)


def backward_body(
    latent_cot, back_own_in, back_low, back_high, edge_cot, weights_in, gain, sender, receiver, exports, slope, y, scale,
    inner, z, nscale, count,
    back_before, back_own, back_after, dh_out, dbefore_out, drim_out, dq_out, dinner_out, cot_out,
    held, sems,
):
    weights = Fetch(weights_in, 0, BACKWARD_ORDER, held, sems)
    nodes = latent_cot.shape[0]
    cot16 = add_returned(
        latent_cot[...], back_own_in[...], back_low[...], back_high[...], exports[...]
    )
    cot_out[...] = cot16
    dq, dinner, dsum = nodes_backward(
        0, cot16.astype(F32), inner[...], z[...], nscale[...][:, 0:1], weights, gain
    )
    dq_out[...] = dq
    dinner_out[...] = dinner
    edges_backward(
        0, dsum, edge_cot, slope, y, scale, weights, gain, receiver, count, dh_out, dbefore_out
    )
    drim_out[...] = halo_back(
        dbefore_out, sender, weights, nodes, (back_before, back_own, back_after)
    )


def finish_body(latent_cot, back_own_in, back_low, back_high, exports, out):
    out[...] = add_returned(
        latent_cot[...], back_own_in[...], back_low[...], back_high[...], exports[...]
    )


def neighbours(axis, wrap):
    size = lax.axis_size(axis)
    up = [(i, (i + 1) % size) for i in range(size if wrap else size - 1)]
    return up, [(j, i) for i, j in up]


def stack_body(low, own, high, out):
    rows = own.shape[0]
    for v, ref in enumerate((low, own, high)):
        out[v * rows : (v + 1) * rows] = ref[...]


def combine_body(own, from_before, from_after, low_out, own_out, high_out):
    rows = own_out.shape[0]
    total = own[...].astype(F32) + from_before[...].astype(F32) + from_after[...].astype(F32)
    low_out[...] = total[:rows].astype(BF16)
    own_out[...] = total[rows : 2 * rows]
    high_out[...] = total[2 * rows :].astype(BF16)


def exchange(rows, work):
    up, down = neighbours("lat", True)
    parts = (lax.ppermute(rows, "lat", up), rows, lax.ppermute(rows, "lat", down))
    parts, done = lax.optimization_barrier((parts, work()))
    kind = shape((3 * rows.shape[0], rows.shape[1]), BF16)
    (bands,) = call(stack_body, "stack", [(p, "v") for p in parts], (kind,))
    up, down = neighbours("lon", True)
    return (lax.ppermute(bands, "lon", up), bands, lax.ppermute(bands, "lon", down)), done


def give_back(before, own, after, held=None):
    up, down = neighbours("lon", True)
    from_before = lax.ppermute(after, "lon", up)
    from_after = lax.ppermute(before, "lon", down)
    rows = own.shape[0] // 3
    to_low, kept, to_high = call(
        combine_body, "combine", [(own, "v"), (from_before, "v"), (from_after, "v")],
        (shape((rows, own.shape[1]), BF16), shape((rows, own.shape[1]), F32),
         shape((rows, own.shape[1]), BF16)),
    )
    up, down = neighbours("lat", True)
    to_low, to_high, held = lax.optimization_barrier((to_low, to_high, held))
    low = lax.ppermute(to_high, "lat", up)
    high = lax.ppermute(to_low, "lat", down)
    return (kept, low, high), held


def join_body(rows_of, keep0, other0, keep1, other1, out, held, sems):
    halves, bands, tall, width = keep0.shape
    lap = 2 * (tall - rows_of)
    copies = []
    for h in range(halves):
        for band in range(bands):
            first = keep0[h, band].astype(F32) + other0[h, band].astype(F32)
            second = keep1[h, band].astype(F32) + other1[h, band].astype(F32)
            middle = first[tall - lap :] + second[:lap]
            block = jnp.concatenate([first[: tall - lap], middle, second[lap:]], axis=0)
            held[h * bands + band] = block.astype(BF16)
        part = pl.ds(h * bands, bands)
        copies.append(pltpu.make_async_copy(held.at[part], out.at[part], sems.at[h]))
        copies[-1].start()
    for copy in copies:
        copy.wait()


def swap_cores(send):
    sectors = lax.axis_size("lon")
    return lax.ppermute(send, "lon", [(i, i ^ 1) for i in range(sectors)])


def reduce_pieces(joined):
    sectors, bands = lax.axis_size("lon"), lax.axis_size("lat")
    groups = [
        [(2 * s + c) * bands + b for s in range(sectors // 2) for b in range(bands)]
        for c in range(2)
    ]
    pieces = lax.all_to_all(
        joined, ("lon", "lat"), 0, 0, axis_index_groups=groups, tiled=True
    )
    return jnp.sum(pieces.astype(F32), axis=0).reshape(2, 1, -1)


def shards(
    grid_state, grid_weight, encode_weights, encode_bias, mesh_gain, g2m_sender, g2m_receiver,
    edge_geometry, edge_embed, mesh_sender, mesh_receiver, block_count, export_nodes, proc_weights,
    proc_bias, proc_gain, mesh_cotangent,
):
    nodes, width = mesh_cotangent.shape[2:]
    sectors, bands = lax.axis_size("lon"), lax.axis_size("lat")
    sender, receiver, exports = mesh_sender[0], mesh_receiver[0], export_nodes[0]
    edges, exported = sender.shape[1], exports.shape[1]
    cotangent = mesh_cotangent[0, 0]
    node16 = shape((nodes, width), BF16)
    node32 = shape((nodes, width), F32)
    edge16 = shape((edges, width), BF16)
    edge32 = shape((edges, width), F32)
    rows16 = shape((exported, width), BF16)
    band16 = shape((3 * exported, width), BF16)
    slots16 = shape((9 * exported, width), BF16)
    scale32 = shape((edges, 128), F32)
    rows_of = MATRICES * width // (sectors * bands)
    tall = -(-rows_of // 16) * 16
    half16 = shape((sectors // 2, bands, tall, width), BF16)

    sources = (
        jnp.swapaxes(grid_state[0, 0], 0, 1), grid_weight, encode_weights, encode_bias[None], mesh_gain[None],
        g2m_sender[0], g2m_receiver[0], exports,
    )
    latent0, export0 = call(
        encode_body, "encode", [(a, "h") for a in sources], (node16, rows16),
        scratch=[pltpu.VMEM(a.shape, a.dtype) for a in sources] + [pltpu.SemaphoreType.DMA((8,))],
        limit=56, flops=6 * 10**9,
    )
    def weight_grads_of(step, latent, halo, node_sum, nact, edge_state, act, dq, dinner, dh, dbefore,
                        drim, cot):
        order = (0, 4, 2, 1) if step else (4, 2, 1)
        return call(
            partial(weights_body, step), "weights",
            [(a, "v") for a in (latent,) + halo + (node_sum, nact, edge_state, act, dq, dinner, dh,
                                                  dbefore, drim)]
            + [(proc_weights, "h"), (sender, "v"), (receiver, "v"), (cot, "v")],
            (half16, half16) + ((edge16,) if step else ()) + (node32,),
            out_kinds="aa" + ("v" if step else "") + "v",
            scratch=fetch_scratch(order, width) + (
                pltpu.VMEM((MATRICES * width + 16, width), F32),
                pltpu.VMEM((2,) + half16.shape, BF16),
                pltpu.SemaphoreType.DMA((sectors,)),
            ),
            flops=6 * 10**9,
        )

    shared = [(proc_weights, "h"), (proc_bias, "v"), (sender, "v"), (receiver, "v")]
    halo0, (edge0, pre0) = exchange(export0, lambda: call(
        first_pre_body, "first_pre",
        [(edge_geometry[0, 0], "v"), (edge_embed, "v"), (latent0, "v")] + shared,
        (edge16, edge32), scratch=fetch_scratch(PRE_ORDER, width), flops=5 * 10**9,
    ))
    (latent1, export1, edge1, slope0, act0, y0, scale0, sum0, inner0, nact0, z0, nscale0) = call(
        forward_body, "forward",
        [(pre0, "v")] + [(h, "v") for h in halo0]
        + [(latent0, "v"), (edge0, "v"), (proc_weights, "h"), (proc_bias, "v"), (proc_gain, "v"),
           (sender, "v"), (receiver, "v"), (exports, "v"), (block_count, "s")],
        (node16, rows16, edge16, edge16, edge16, edge16, scale32, node16, node32, node16, node32,
         shape((nodes, 128), F32)),
        scratch=fetch_scratch(FORWARD_ORDER, width),
    )
    halo1, (pre1,) = exchange(export1, lambda: call(
        partial(pre_body, 1), "pre", [(latent1, "v"), (edge1, "v")] + shared, (edge32,),
        scratch=fetch_scratch(PRE_ORDER, width), flops=3 * 10**9,
    ))
    (latent2, before1, own1, after1, act1, dh1, dbefore1, drim1, sum1, nact1, dq1, dinner1) = call(
        last_body, "last",
        [(pre1, "v")] + [(h, "v") for h in halo1]
        + [(latent1, "v"), (proc_weights, "h"), (proc_bias, "v"), (proc_gain, "v"), (sender, "v"),
           (receiver, "v"), (cotangent, "v"), (block_count, "s")],
        (node16, band16, band16, band16, edge16, edge16, edge16, slots16, node16, node16, node16,
         node16),
        scratch=(pltpu.VMEM((edges, width), BF16), pltpu.VMEM((edges, width), BF16),
                 pltpu.VMEM((edges, 128), F32)) + fetch_scratch(LAST_ORDER, width),
    )
    returned1, _ = give_back(before1, own1, after1)
    keep1, send1, edge_cot1, latent_cot1 = weight_grads_of(
        1, latent1, halo1, sum1, nact1, edge1, act1, dq1, dinner1, dh1, dbefore1, drim1, cotangent
    )
    other1 = swap_cores(send1)
    (before0, own0, after0, dh0, dbefore0, drim0, dq0, dinner0, cot0) = call(
        backward_body, "backward",
        [(latent_cot1, "v")] + [(r, "v") for r in returned1] + [(edge_cot1, "v"), (proc_weights, "h"),
         (proc_gain, "v"), (sender, "v"), (receiver, "v"), (exports, "v"), (slope0, "v"),
         (y0, "v"), (scale0, "v"), (inner0, "v"), (z0, "v"), (nscale0, "v"), (block_count, "s")],
        (band16, band16, band16, edge16, edge16, slots16, node16, node16, node16),
        scratch=fetch_scratch(BACKWARD_ORDER, width),
    )
    keep0, send0, latent_cot0 = weight_grads_of(
        0, latent0, halo0, sum0, nact0, edge0, act0, dq0, dinner0, dh0, dbefore0, drim0, cot0
    )
    returned0, send0 = give_back(before0, own0, after0, send0)
    other0 = swap_cores(send0)
    (joined,) = call(
        partial(join_body, rows_of), "join",
        [(keep0, "v"), (other0, "v"), (keep1, "v"), (other1, "v")],
        (shape((sectors // 2 * bands, 2 * rows_of, width), BF16),), out_kinds="a",
        scratch=(pltpu.VMEM((sectors // 2 * bands, 2 * rows_of, width), BF16),
                 pltpu.SemaphoreType.DMA((sectors // 2,))),
        limit=44,
    )
    joined, returned0 = lax.optimization_barrier((joined, returned0))
    weight_grads = reduce_pieces(joined)
    (latent_grad,) = call(
        finish_body, "finish", [(latent_cot0, "v")] + [(r, "v") for r in returned0] + [(exports, "v")], (node16,)
    )
    return latent2[None, None], weight_grads, latent_grad[None, None]


def solution(mesh):
    tile = P("lon", "lat", None)
    deep = P("lon", "lat", None, None)
    return jax.shard_map(
        shards,
        mesh=mesh,
        in_specs=(
            deep, P(), P(), P(), P(), tile, tile, deep, P(), tile, tile, P("lon", "lat"), tile,
            P(), P(), P(), deep,
        ),
        out_specs=(deep, P(None, ("lon", "lat"), None), deep),
        check_vma=False,
    )
```

```python
from functools import partial

import jax
import jax.numpy as jnp
from jax import lax
from jax.experimental import pallas as pl
from jax.experimental.pallas import tpu as pltpu
from jax.sharding import PartitionSpec as P

EDGE_BLOCK = 256
EPSILON = 1e-05
F32 = jnp.float32
BF16 = jnp.bfloat16
HIGHEST = lax.Precision.HIGHEST


def dot(a, b):
    return jnp.dot(a, b, preferred_element_type=F32)


def dot_nt(a, b):
    return lax.dot_general(a, b, (((1,), (1,)), ((), ())), preferred_element_type=F32)


def dot_tn(a, b):
    return lax.dot_general(a, b, (((0,), (0,)), ((), ())), preferred_element_type=F32)


def gate(v):
    return 0.5 * jnp.tanh(0.5 * v) + 0.5


def silu(v):
    return v * gate(v)


def silu_slope(v):
    s = gate(v)
    return s * (1.0 + v * (1.0 - s))


def norm(v):
    mean = jnp.mean(v, axis=-1, keepdims=True)
    centred = v - mean
    variance = jnp.mean(centred * centred, axis=-1, keepdims=True)
    scale = lax.rsqrt(variance + EPSILON)
    return centred * scale, scale


def norm_back(g, y, scale):
    first = jnp.mean(g, axis=-1, keepdims=True)
    second = jnp.mean(g * y, axis=-1, keepdims=True)
    return scale * (g - first - y * second)


def ids_down(row, count, base=0):
    shape = (count, row.shape[1])
    numbers = (lax.broadcasted_iota(jnp.int32, shape, 0) + base).astype(F32)
    return jnp.where(numbers == row.astype(F32), 1.0, 0.0).astype(BF16)


def ids_across(row, count, base=0):
    edges = row.shape[1]
    column = jnp.transpose(jnp.broadcast_to(row.astype(F32), (128, edges)))
    parts = []
    lane = lax.broadcasted_iota(jnp.int32, (edges, 128), 1).astype(F32)
    for start in range(0, count, 128):
        width = min(128, count - start)
        hit = jnp.where(column == lane + float(start + base), 1.0, 0.0)
        parts.append(hit[:, :width])
    return jnp.concatenate(parts, axis=1).astype(BF16)


VMEM_SPEC = pl.BlockSpec(memory_space=pltpu.VMEM)
SMEM_SPEC = pl.BlockSpec(memory_space=pltpu.SMEM)
HBM_SPEC = pl.BlockSpec(memory_space=pltpu.HBM)
ANY_SPEC = pl.BlockSpec(memory_space=pl.ANY)
SPECS = {"v": VMEM_SPEC, "s": SMEM_SPEC, "h": HBM_SPEC, "a": ANY_SPEC}
MATRICES = 7


def call(body, name, args, outs, scratch=(), out_kinds=None, limit=24, flops=10**6):
    out_kinds = out_kinds or "v" * len(outs)
    return pl.pallas_call(
        body,
        out_shape=tuple(outs),
        in_specs=[SPECS[kind] for _, kind in args],
        out_specs=tuple(SPECS[kind] for kind in out_kinds),
        scratch_shapes=list(scratch),
        compiler_params=pltpu.CompilerParams(vmem_limit_bytes=limit << 20),
        cost_estimate=pl.CostEstimate(flops=flops, bytes_accessed=10**5, transcendentals=0),
        name=name,
    )(*[a for a, _ in args])


def shape(dims, dtype):
    return jax.ShapeDtypeStruct(dims, dtype)


class Matrices:
    def __init__(self, source, step):
        self.source = source
        self.step = step

    def __getitem__(self, m):
        return self.source[self.step, m]


def encode_body(
    grid_in, gw_in, ew_in, eb_in, gain_in, sender_in, receiver_in, exports_in,
    latent_out, export_out,
    grid, gw, ew, eb, gain, sender, receiver, exports, sems,
):
    pairs = [
        (grid_in, grid), (gw_in, gw), (sender_in, sender), (ew_in, ew), (eb_in, eb),
        (receiver_in, receiver), (gain_in, gain), (exports_in, exports),
    ]
    copies = [pltpu.make_async_copy(a, b, sems.at[i]) for i, (a, b) in enumerate(pairs)]
    for copy in copies:
        copy.start()
    copies[0].wait()
    copies[1].wait()
    cells = grid.shape[1]
    nodes = latent_out.shape[0]
    latent = silu(dot_tn(grid[...], gw[...])).astype(BF16)
    for copy in copies[2:]:
        copy.wait()
    total = jnp.zeros(latent_out.shape, F32)
    edges = sender.shape[1]
    for start in range(0, edges, 256):
        part = slice(start, start + 256)
        picked = dot(ids_across(sender[:, part], cells), latent).astype(BF16)
        act = silu(dot(picked, ew[0]) + eb[...]).astype(BF16)
        message = dot(act, ew[1]).astype(BF16)
        total = total + dot(ids_down(receiver[:, part], nodes), message)
    value = (norm(total)[0] * gain[...]).astype(BF16)
    latent_out[...] = value
    export_out[...] = dot_tn(ids_down(exports[...], nodes), value).astype(BF16)


def embed_edges(geometry, embed):
    features, edges = geometry.shape
    columns = [
        jnp.transpose(jnp.broadcast_to(geometry[f : f + 1], (128, edges))) for f in range(features)
    ]
    parts = []
    for start in range(0, embed.shape[1], 128):
        total = columns[0] * embed[0:1, start : start + 128]
        for f in range(1, features):
            total = total + columns[f] * embed[f : f + 1, start : start + 128]
        parts.append(total)
    return jnp.concatenate(parts, axis=1)


def first_pre_body(
    geometry, embed, latent, weights_in, bias, sender, receiver, edge_out, pre_out
):
    values = embed[...]
    for start in range(0, sender.shape[1], EDGE_BLOCK):
        part = slice(start, start + EDGE_BLOCK)
        edge_out[part] = embed_edges(geometry[:, part], values).astype(BF16)
    pre_body(0, latent, edge_out, weights_in, bias, sender, receiver, pre_out)


def pre_body(step, latent, edge_state, weights_in, bias, sender, receiver, pre_out):
    weights = Matrices(weights_in, step)
    nodes = latent.shape[0]
    rows = latent[...]
    own = jnp.concatenate([dot(rows, weights[1]), dot(rows, weights[2])], axis=0).astype(BF16)
    for start in range(0, sender.shape[1], EDGE_BLOCK):
        part = slice(start, start + EDGE_BLOCK)
        picks = jnp.concatenate(
            [ids_across(sender[:, part], nodes), ids_across(receiver[:, part], nodes)], axis=1
        )
        pre_out[part] = dot(edge_state[part], weights[0]) + dot(picks, own) + bias[step, 0:1]


def band_masks():
    band = lax.axis_index("lat")
    return (band > 0).astype(F32), (band < lax.axis_size("lat") - 1).astype(F32)


def halo_rows(before, own, after):
    count = before.shape[0] // 3
    low, high = (mask.astype(BF16) for mask in band_masks())
    parts = []
    for v, mask in ((0, low), (1, None), (2, high)):
        for ref in (before, own, after):
            rows = ref[v * count : (v + 1) * count]
            parts.append(rows if mask is None else rows * mask)
    return jnp.concatenate(parts, axis=0)


def edges_forward(
    step, pre, halo, weights, gain, sender, receiver, count, slope_out, act_out, y_out, scale_out, nodes,
    edges=None,
):
    rim = dot(halo, weights[1]).astype(BF16)
    blocks = sender.shape[1] // EDGE_BLOCK
    parts = [slice(b * EDGE_BLOCK, (b + 1) * EDGE_BLOCK) for b in range(blocks)]
    total = jnp.zeros((nodes, halo.shape[1]), F32)
    before, hidden, update = {}, {}, {}

    def project(b):
        before[b] = dot(ids_across(sender[:, parts[b]], halo.shape[0], nodes), rim)

    def activate(b):
        value = pre[parts[b]] + before.pop(b)
        share = gate(value)
        product = value * share
        slope_out[parts[b]] = (share + product - product * share).astype(BF16)
        act_out[parts[b]] = product.astype(BF16)

    def multiply(b):
        hidden[b] = dot(act_out[parts[b]], weights[3])

    def finish(b):
        live = (b < count[0, 0]).astype(F32)
        y, scale = norm(hidden.pop(b))
        y_out[parts[b]] = y.astype(BF16)
        scale_out[parts[b]] = jnp.broadcast_to(scale, (EDGE_BLOCK, 128))
        value = y * (gain[step, 0:1] * live)
        update[b] = value.astype(BF16)
        if edges is not None:
            edges[1][parts[b]] = (edges[0][parts[b]].astype(F32) + value).astype(BF16)

    project(0)
    for b in range(blocks + 2):
        if b + 1 < blocks:
            project(b + 1)
        if b < blocks:
            activate(b)
        if 1 <= b <= blocks:
            finish(b - 1) if b - 1 in hidden else None
        if b < blocks:
            multiply(b)
        if b >= 1 and b - 1 in update:
            total = total + dot(ids_down(receiver[:, parts[b - 1]], nodes), update.pop(b - 1))
    return total.astype(BF16)


def nodes_forward(step, latent, node_sum, weights, bias, gain):
    inner = dot(latent, weights[4]) + dot(node_sum, weights[5]) + bias[step, 1:2]
    act = silu(inner).astype(BF16)
    z, scale = norm(dot(act, weights[6]))
    return inner, act, z, scale, latent.astype(F32) + z * gain[step, 1:2]


def forward_body(
    pre, halo_before, halo_own, halo_after, latent, edge_state, weights_in, bias, gain, sender,
    receiver, exports, count,
    latent_out, export_out, edges_out, slope_out, act_out, y_out, scale_out,
    sum_out, inner_out, nact_out, z_out, nscale_out,
):
    weights = Matrices(weights_in, 0)
    nodes = latent.shape[0]
    halo = halo_rows(halo_before, halo_own, halo_after)
    node_sum = edges_forward(
        0, pre, halo, weights, gain, sender, receiver, count, slope_out, act_out, y_out, scale_out,
        nodes, (edge_state, edges_out),
    )
    inner, act, z, scale, new = nodes_forward(0, latent[...], node_sum, weights, bias, gain)
    value = new.astype(BF16)
    latent_out[...] = value
    export_out[...] = dot_tn(ids_down(exports[...], nodes), value).astype(BF16)
    sum_out[...] = node_sum
    inner_out[...] = inner
    nact_out[...] = act
    z_out[...] = z
    nscale_out[...] = jnp.broadcast_to(scale, nscale_out.shape)


def nodes_backward(step, cot, inner, z, scale, weights, gain):
    dq = norm_back(cot * gain[step, 1:2], z, scale).astype(BF16)
    dact = dot_nt(dq, weights[6]).astype(BF16).astype(F32)
    dinner = (dact * silu_slope(inner)).astype(BF16)
    dsum = dot_nt(dinner, weights[5]).astype(BF16)
    return dq, dinner, dsum


def edges_backward(
    step, dsum, edge_cot, slope, y, scale, weights, gain, receiver, count, dh_out, dbefore_out
):
    nodes = dsum.shape[0]
    blocks = receiver.shape[1] // EDGE_BLOCK
    parts = [slice(b * EDGE_BLOCK, (b + 1) * EDGE_BLOCK) for b in range(blocks)]
    cots, dacts = {}, {}

    def spread(b):
        cots[b] = dot(ids_across(receiver[:, parts[b]], nodes), dsum)

    def through_norm(b):
        live = (b < count[0, 0]).astype(F32)
        cot = cots.pop(b)
        if edge_cot is not None:
            cot = cot + edge_cot[parts[b]].astype(F32)
        dh = norm_back(
            cot * (gain[step, 0:1] * live), y[parts[b]].astype(F32), scale[parts[b]][:, 0:1]
        )
        dh_out[parts[b]] = dh.astype(BF16)

    def multiply(b):
        dacts[b] = dot_nt(dh_out[parts[b]], weights[3])

    def finish(b):
        dact = dacts.pop(b).astype(BF16).astype(F32)
        dbefore_out[parts[b]] = (dact * slope[parts[b]].astype(F32)).astype(BF16)

    spread(0)
    for b in range(blocks + 1):
        if b + 1 < blocks:
            spread(b + 1)
        if b < blocks:
            through_norm(b)
        if b >= 1:
            finish(b - 1)
        if b < blocks:
            multiply(b)


def halo_back(dbefore, sender, weights, nodes, outs):
    rows = outs[0].shape[0] // 3
    slots = 9 * rows
    total = jnp.zeros((slots, dbefore.shape[1]), F32)
    for block in range(sender.shape[1] // EDGE_BLOCK):
        part = slice(block * EDGE_BLOCK, (block + 1) * EDGE_BLOCK)
        total = total + dot(ids_down(sender[:, part], slots, nodes), dbefore[part])
    total = total.astype(BF16)
    grad = dot_nt(total, weights[1]).astype(BF16)
    for v in range(3):
        for w in range(3):
            g = 3 * v + w
            outs[w][v * rows : (v + 1) * rows] = grad[g * rows : (g + 1) * rows]
    return total


def last_body(
    pre, halo_before, halo_own, halo_after, latent, weights_in, bias, gain, sender, receiver,
    cotangent, count,
    latent_out, back_before, back_own, back_after, act_out, dh_out, dbefore_out, drim_out, sum_out,
    nact_out, dq_out, dinner_out,
    slope, y, scale,
):
    weights = Matrices(weights_in, 1)
    nodes = latent.shape[0]
    halo = halo_rows(halo_before, halo_own, halo_after)
    node_sum = edges_forward(
        1, pre, halo, weights, gain, sender, receiver, count, slope, act_out, y, scale, nodes
    )
    inner, nact, z, nscale, new = nodes_forward(1, latent[...], node_sum, weights, bias, gain)
    latent_out[...] = new.astype(BF16)
    sum_out[...] = node_sum
    nact_out[...] = nact
    dq, dinner, dsum = nodes_backward(
        1, cotangent[...].astype(F32), inner, z, nscale, weights, gain
    )
    dq_out[...] = dq
    dinner_out[...] = dinner
    edges_backward(
        1, dsum, None, slope, y, scale, weights, gain, receiver, count, dh_out, dbefore_out
    )
    drim_out[...] = halo_back(
        dbefore_out, sender, weights, nodes, (back_before, back_own, back_after)
    )


def weights_body(
    step, latent, halo_before, halo_own, halo_after, node_sum, nact, edge_state, act, dq, dinner, dh,
    dbefore, drim, weights_in, sender, receiver, cotangent, *rest,
):
    if step:
        keep_out, send_out, edge_cot_out, latent_cot_out = rest[:4]
    else:
        keep_out, send_out, latent_cot_out = rest[:3]
    total, pieces, piece_sems = rest[-3:]
    weights = Matrices(weights_in, step)
    nodes, width = latent.shape
    halves, bands, tall = pieces.shape[1:4]
    rows_of = MATRICES * width // (2 * halves * bands)
    mine = lax.axis_index("lon") % 2
    copies = []
    emitted = 0

    spare = tall - rows_of
    number = lax.broadcasted_iota(jnp.int32, (tall, width), 0)
    inside = number >= spare if step else number < rows_of
    edge = jnp.zeros((8, width), F32)
    total[:8] = edge
    total[8 + MATRICES * width :] = edge

    def put(matrix, value):
        nonlocal emitted
        total[8 + matrix * width : 8 + (matrix + 1) * width] = value
        ready = (matrix + 1) * width + (spare if matrix == MATRICES - 1 else 0)
        while emitted < 2 * halves and ((emitted + 1) * bands - 1) * rows_of + tall <= ready:
            for band in range(bands):
                first = 8 + (emitted * bands + band) * rows_of - (spare if step else 0)
                rows = jnp.where(inside, total[first : first + tall], 0.0)
                pieces[emitted % 2, emitted // 2, band] = rows.astype(BF16)
            emitted += 1
            if emitted % 2 == 0:
                h = emitted // 2 - 1
                for place, out in ((mine, keep_out), (1 - mine, send_out)):
                    copy = pltpu.make_async_copy(
                        pieces.at[place, h], out.at[h], piece_sems.at[len(copies)]
                    )
                    copy.start()
                    copies.append(copy)

    rows = latent[...]
    put(0, dot_tn(edge_state[...], dbefore[...]))
    dsend = jnp.zeros((nodes, width), F32)
    drecv = jnp.zeros((nodes, width), F32)
    for block in range(sender.shape[1] // EDGE_BLOCK):
        part = slice(block * EDGE_BLOCK, (block + 1) * EDGE_BLOCK)
        dsend = dsend + dot(ids_down(sender[:, part], nodes), dbefore[part])
        drecv = drecv + dot(ids_down(receiver[:, part], nodes), dbefore[part])
    dsend = dsend.astype(BF16)
    drecv = drecv.astype(BF16)
    halo = halo_rows(halo_before, halo_own, halo_after)
    put(1, dot_tn(rows, dsend) + dot_tn(halo, drim[...]))
    put(2, dot_tn(rows, drecv))
    put(3, dot_tn(act[...], dh[...]))
    put(4, dot_tn(rows, dinner[...]))
    put(5, dot_tn(node_sum[...], dinner[...]))
    put(6, dot_tn(nact[...], dq[...]))
    if step:
        edge_cot_out[...] = dot_nt(dbefore[...], weights[0]).astype(BF16)
    own = (
        dot_nt(dinner[...], weights[4]).astype(BF16).astype(F32)
        + dot_nt(drecv, weights[2]).astype(BF16).astype(F32)
    ).astype(BF16).astype(F32)
    latent_cot_out[...] = (
        cotangent[...].astype(F32) + own + dot_nt(dsend, weights[1]).astype(BF16).astype(F32)
    )
    for copy in copies:
        copy.wait()


def add_returned(cot, own, before, after, exports):
    spots = ids_down(exports, cot.shape[0]).astype(F32)
    low, high = band_masks()
    returned = own + before.astype(F32) * low + after.astype(F32) * high
    extra = jnp.dot(spots, returned, precision=HIGHEST, preferred_element_type=F32)
    return (cot + extra).astype(BF16)


def backward_body(
    latent_cot, back_own_in, back_low, back_high, edge_cot, weights_in, gain, sender, receiver, exports, slope, y, scale,
    inner, z, nscale, count,
    back_before, back_own, back_after, dh_out, dbefore_out, drim_out, dq_out, dinner_out, cot_out,
):
    weights = Matrices(weights_in, 0)
    nodes = latent_cot.shape[0]
    cot16 = add_returned(
        latent_cot[...], back_own_in[...], back_low[...], back_high[...], exports[...]
    )
    cot_out[...] = cot16
    dq, dinner, dsum = nodes_backward(
        0, cot16.astype(F32), inner[...], z[...], nscale[...][:, 0:1], weights, gain
    )
    dq_out[...] = dq
    dinner_out[...] = dinner
    edges_backward(
        0, dsum, edge_cot, slope, y, scale, weights, gain, receiver, count, dh_out, dbefore_out
    )
    drim_out[...] = halo_back(
        dbefore_out, sender, weights, nodes, (back_before, back_own, back_after)
    )


def finish_body(latent_cot, back_own_in, back_low, back_high, exports, out):
    out[...] = add_returned(
        latent_cot[...], back_own_in[...], back_low[...], back_high[...], exports[...]
    )


def neighbours(axis, wrap):
    size = lax.axis_size(axis)
    up = [(i, (i + 1) % size) for i in range(size if wrap else size - 1)]
    return up, [(j, i) for i, j in up]


def stack_body(low, own, high, out):
    rows = own.shape[0]
    for v, ref in enumerate((low, own, high)):
        out[v * rows : (v + 1) * rows] = ref[...]


def combine_body(own, from_before, from_after, low_out, own_out, high_out):
    rows = own_out.shape[0]
    total = own[...].astype(F32) + from_before[...].astype(F32) + from_after[...].astype(F32)
    low_out[...] = total[:rows].astype(BF16)
    own_out[...] = total[rows : 2 * rows]
    high_out[...] = total[2 * rows :].astype(BF16)


def exchange(rows, work):
    up, down = neighbours("lat", True)
    parts = (lax.ppermute(rows, "lat", up), rows, lax.ppermute(rows, "lat", down))
    parts, done = lax.optimization_barrier((parts, work()))
    kind = shape((3 * rows.shape[0], rows.shape[1]), BF16)
    (bands,) = call(stack_body, "stack", [(p, "v") for p in parts], (kind,))
    up, down = neighbours("lon", True)
    return (lax.ppermute(bands, "lon", up), bands, lax.ppermute(bands, "lon", down)), done


def give_back(before, own, after, held=None):
    up, down = neighbours("lon", True)
    from_before = lax.ppermute(after, "lon", up)
    from_after = lax.ppermute(before, "lon", down)
    rows = own.shape[0] // 3
    to_low, kept, to_high = call(
        combine_body, "combine", [(own, "v"), (from_before, "v"), (from_after, "v")],
        (shape((rows, own.shape[1]), BF16), shape((rows, own.shape[1]), F32),
         shape((rows, own.shape[1]), BF16)),
    )
    up, down = neighbours("lat", True)
    to_low, to_high, held = lax.optimization_barrier((to_low, to_high, held))
    low = lax.ppermute(to_high, "lat", up)
    high = lax.ppermute(to_low, "lat", down)
    return (kept, low, high), held


def join_body(rows_of, keep0, other0, keep1, other1, out, held, sems):
    halves, bands, tall, width = keep0.shape
    lap = 2 * (tall - rows_of)
    copies = []
    for h in range(halves):
        for band in range(bands):
            first = keep0[h, band].astype(F32) + other0[h, band].astype(F32)
            second = keep1[h, band].astype(F32) + other1[h, band].astype(F32)
            middle = first[tall - lap :] + second[:lap]
            block = jnp.concatenate([first[: tall - lap], middle, second[lap:]], axis=0)
            held[h * bands + band] = block.astype(BF16)
        part = pl.ds(h * bands, bands)
        copies.append(pltpu.make_async_copy(held.at[part], out.at[part], sems.at[h]))
        copies[-1].start()
    for copy in copies:
        copy.wait()


def swap_cores(send):
    sectors = lax.axis_size("lon")
    return lax.ppermute(send, "lon", [(i, i ^ 1) for i in range(sectors)])


def reduce_pieces(joined):
    sectors, bands = lax.axis_size("lon"), lax.axis_size("lat")
    groups = [
        [(2 * s + c) * bands + b for s in range(sectors // 2) for b in range(bands)]
        for c in range(2)
    ]
    pieces = lax.all_to_all(
        joined, ("lon", "lat"), 0, 0, axis_index_groups=groups, tiled=True
    )
    return jnp.sum(pieces.astype(F32), axis=0).reshape(2, 1, -1)


def shards(
    grid_state, grid_weight, encode_weights, encode_bias, mesh_gain, g2m_sender, g2m_receiver,
    edge_geometry, edge_embed, mesh_sender, mesh_receiver, block_count, export_nodes, proc_weights,
    proc_bias, proc_gain, mesh_cotangent,
):
    nodes, width = mesh_cotangent.shape[2:]
    sectors, bands = lax.axis_size("lon"), lax.axis_size("lat")
    sender, receiver, exports = mesh_sender[0], mesh_receiver[0], export_nodes[0]
    edges, exported = sender.shape[1], exports.shape[1]
    cotangent = mesh_cotangent[0, 0]
    node16 = shape((nodes, width), BF16)
    node32 = shape((nodes, width), F32)
    edge16 = shape((edges, width), BF16)
    edge32 = shape((edges, width), F32)
    rows16 = shape((exported, width), BF16)
    band16 = shape((3 * exported, width), BF16)
    slots16 = shape((9 * exported, width), BF16)
    scale32 = shape((edges, 128), F32)
    rows_of = MATRICES * width // (sectors * bands)
    tall = -(-rows_of // 16) * 16
    half16 = shape((sectors // 2, bands, tall, width), BF16)

    sources = (
        jnp.swapaxes(grid_state[0, 0], 0, 1), grid_weight, encode_weights, encode_bias[None], mesh_gain[None],
        g2m_sender[0], g2m_receiver[0], exports,
    )
    latent0, export0 = call(
        encode_body, "encode", [(a, "h") for a in sources], (node16, rows16),
        scratch=[pltpu.VMEM(a.shape, a.dtype) for a in sources] + [pltpu.SemaphoreType.DMA((8,))],
        limit=56, flops=6 * 10**9,
    )
    def weight_grads_of(step, latent, halo, node_sum, nact, edge_state, act, dq, dinner, dh, dbefore,
                        drim, cot):
        return call(
            partial(weights_body, step), "weights",
            [(a, "v") for a in (latent,) + halo + (node_sum, nact, edge_state, act, dq, dinner, dh,
                                                  dbefore, drim)]
            + [(proc_weights, "v"), (sender, "v"), (receiver, "v"), (cot, "v")],
            (half16, half16) + ((edge16,) if step else ()) + (node32,),
            out_kinds="aa" + ("v" if step else "") + "v",
            scratch=(
                pltpu.VMEM((MATRICES * width + 16, width), F32),
                pltpu.VMEM((2,) + half16.shape, BF16),
                pltpu.SemaphoreType.DMA((sectors,)),
            ),
            flops=6 * 10**9,
        )

    shared = [(proc_weights, "v"), (proc_bias, "v"), (sender, "v"), (receiver, "v")]
    halo0, (edge0, pre0) = exchange(export0, lambda: call(
        first_pre_body, "first_pre",
        [(edge_geometry[0, 0], "v"), (edge_embed, "v"), (latent0, "v")] + shared,
        (edge16, edge32), flops=5 * 10**9,
    ))
    (latent1, export1, edge1, slope0, act0, y0, scale0, sum0, inner0, nact0, z0, nscale0) = call(
        forward_body, "forward",
        [(pre0, "v")] + [(h, "v") for h in halo0]
        + [(latent0, "v"), (edge0, "v"), (proc_weights, "v"), (proc_bias, "v"), (proc_gain, "v"),
           (sender, "v"), (receiver, "v"), (exports, "v"), (block_count, "s")],
        (node16, rows16, edge16, edge16, edge16, edge16, scale32, node16, node32, node16, node32,
         shape((nodes, 128), F32)),
    )
    halo1, (pre1,) = exchange(export1, lambda: call(
        partial(pre_body, 1), "pre", [(latent1, "v"), (edge1, "v")] + shared, (edge32,),
        flops=3 * 10**9,
    ))
    (latent2, before1, own1, after1, act1, dh1, dbefore1, drim1, sum1, nact1, dq1, dinner1) = call(
        last_body, "last",
        [(pre1, "v")] + [(h, "v") for h in halo1]
        + [(latent1, "v"), (proc_weights, "v"), (proc_bias, "v"), (proc_gain, "v"), (sender, "v"),
           (receiver, "v"), (cotangent, "v"), (block_count, "s")],
        (node16, band16, band16, band16, edge16, edge16, edge16, slots16, node16, node16, node16,
         node16),
        scratch=(pltpu.VMEM((edges, width), BF16), pltpu.VMEM((edges, width), BF16),
                 pltpu.VMEM((edges, 128), F32)),
    )
    returned1, _ = give_back(before1, own1, after1)
    keep1, send1, edge_cot1, latent_cot1 = weight_grads_of(
        1, latent1, halo1, sum1, nact1, edge1, act1, dq1, dinner1, dh1, dbefore1, drim1, cotangent
    )
    other1 = swap_cores(send1)
    (before0, own0, after0, dh0, dbefore0, drim0, dq0, dinner0, cot0) = call(
        backward_body, "backward",
        [(latent_cot1, "v")] + [(r, "v") for r in returned1] + [(edge_cot1, "v"), (proc_weights, "v"),
         (proc_gain, "v"), (sender, "v"), (receiver, "v"), (exports, "v"), (slope0, "v"),
         (y0, "v"), (scale0, "v"), (inner0, "v"), (z0, "v"), (nscale0, "v"), (block_count, "s")],
        (band16, band16, band16, edge16, edge16, slots16, node16, node16, node16),
    )
    keep0, send0, latent_cot0 = weight_grads_of(
        0, latent0, halo0, sum0, nact0, edge0, act0, dq0, dinner0, dh0, dbefore0, drim0, cot0
    )
    returned0, send0 = give_back(before0, own0, after0, send0)
    other0 = swap_cores(send0)
    (joined,) = call(
        partial(join_body, rows_of), "join",
        [(keep0, "v"), (other0, "v"), (keep1, "v"), (other1, "v")],
        (shape((sectors // 2 * bands, 2 * rows_of, width), BF16),), out_kinds="a",
        scratch=(pltpu.VMEM((sectors // 2 * bands, 2 * rows_of, width), BF16),
                 pltpu.SemaphoreType.DMA((sectors // 2,))),
        limit=44,
    )
    joined, returned0 = lax.optimization_barrier((joined, returned0))
    weight_grads = reduce_pieces(joined)
    (latent_grad,) = call(
        finish_body, "finish", [(latent_cot0, "v")] + [(r, "v") for r in returned0] + [(exports, "v")], (node16,)
    )
    return latent2[None, None], weight_grads, latent_grad[None, None]


def solution(mesh):
    tile = P("lon", "lat", None)
    deep = P("lon", "lat", None, None)
    return jax.shard_map(
        shards,
        mesh=mesh,
        in_specs=(
            deep, P(), P(), P(), P(), tile, tile, deep, P(), tile, tile, P("lon", "lat"), tile,
            P(), P(), P(), deep,
        ),
        out_specs=(deep, P(None, ("lon", "lat"), None), deep),
        check_vma=False,
    )
```
